256 devices in a mesh: ex: 32 (over z, y_hi, core), grp: 8 (over y_lo, x).
Axes of the slice: x: 4, y: 4 (y_hi: 2, y_lo: 2; y = y_hi * 2 + y_lo), z: 8, core: 2. Of those that a mesh axis runs over, the one named last changes fastest.
Arguments:
- queries: bfloat16 [8192, 65536], P('ex', 'grp'), may hold values from -6 to 6
- inv_in: bfloat16 [16, 64, 64], P('grp'), as said below
- inv_out: bfloat16 [16, 64, 64], P('grp'), as said below
- store: bfloat16 [16384, 65536], P('ex', 'grp'), may hold values from -0.0234375 to 0.0234375
- listed: int32 [256, 24], P('ex'), may hold values from 0 to 1, as said below
Outputs:
- scores: float32 [3, 8192, 512], P(None, ('ex', 'grp'))
The draws below stay inside these ranges and needn't reach their ends.
Inputs may be any that keep to these rules, and one draw needn't show every extreme that they name: Entries are 0 or 1; every query block lists column 0 and column 23, the other numbers listed differ from block to block and from ex block to ex block, and some query block lists all 24. `inv_in`: each matrix is symmetric and positive definite. `inv_out`: each matrix is symmetric and positive definite.
All inputs are finite; a program needn't handle non-finite values.
Results may differ from the reference program's by a relative error of at most 0.0041.
Values may be sent and summed in bfloat16 or wider, within the bound.
A program may use at most 64 MiB of HBM per device.

```python
import jax
import jax.numpy as jnp
from jax import lax

R = 64
MODULES = 16
QB = 32
SUB = 64
QRY_DEV = 256
EX_DEV = 512
GD = 65536
SB = 8
QUERIES = 8192
EXAMPLES = 16384
NQB = 256
N_EX = 32


def factor_draw(key):
    base = jax.random.normal(key, (MODULES, R, R), jnp.float32)
    outer = jnp.einsum('mab,mcb->mac', base, base) / R
    return 0.6 * jnp.eye(R, dtype=jnp.float32)[None] + 0.4 * outer


def draw_inv_in(key, part):
    return factor_draw(jax.random.fold_in(key, 11)).astype(jnp.bfloat16)


def draw_inv_out(key, part):
    return factor_draw(jax.random.fold_in(key, 23)).astype(jnp.bfloat16)


def draw_listed(key, part):
    key = jax.random.fold_in(key, 37)
    first, second, third = jax.random.split(key, 3)
    width = 3 * SB
    per_dev = QRY_DEV // QB
    level = jax.random.randint(first, (NQB // per_dev,), 0, width)
    device_level = jnp.repeat(level, per_dev)
    extra = jax.random.randint(second, (NQB,), 0, width)
    counts = jnp.maximum(2, 1 + jnp.minimum(width - 1, (device_level * 3 + extra) // 4))
    counts = counts.at[0].set(width)
    column = jnp.arange(width, dtype=jnp.int32)[None, :]
    scores_int = jax.random.randint(third, (NQB, width), 0, 1 << 20) * width + column
    scores_int = jnp.where(column == 0, -2, jnp.where(column == width - 1, -1, scores_int))
    rank = jnp.argsort(jnp.argsort(scores_int, axis=1), axis=1)
    return (rank < counts[:, None]).astype(jnp.int32)


def block_scale(key, shape, shards, low, top_value):
    def one(position, blocks):
        draws = jax.random.uniform(jax.random.fold_in(jax.random.fold_in(key, 6), position), (blocks,), jnp.float32, low / len(shards), top_value / len(shards))
        return jnp.repeat(jnp.exp(draws), shape[position] // blocks).reshape((-1,) + (1,) * (len(shape) - position - 1))

    factor_of = one(*shards[0])
    for cut in shards[1:]:
        factor_of = factor_of * one(*cut)
    return factor_of


def gaussian(rng, dims, deviation, bound, shards=(), held_as=jnp.bfloat16):
    array = jax.random.normal(rng, dims, jnp.float32) * deviation
    if len(shards) > 0:
        array = block_scale(rng, dims, shards, -0.22, 0.18) * array
    return jnp.clip(array, min=-bound, max=bound).astype(held_as)


def setup_inputs(seed: int = 0) -> dict:
    seeds = jax.random.split(jax.random.key(seed), 6)
    return {
        "queries": gaussian(seeds[0], (QUERIES, GD), 1.0, 6.0, ((0, 32), (1, 8))),
        "inv_in": draw_inv_in(jax.random.fold_in(seeds[5], 71), 0),
        "inv_out": draw_inv_out(jax.random.fold_in(seeds[5], 71), 0),
        "store": gaussian(seeds[3], (EXAMPLES, GD), GD ** -0.5, 0.0234375, ((0, 32), (1, 8))),
        "listed": draw_listed(jax.random.fold_in(seeds[5], 71), 0),
    }


def widen(piece):
    count = piece.shape[1]
    rows = piece.shape[0]
    full = jnp.broadcast_to(piece.astype(jnp.float32)[:, None, :, None], (rows, QB, count, SUB))
    return full.reshape(rows * QB, count * SUB)


def reference(queries, inv_in, inv_out, store, listed):
    inv_left = inv_in.astype(jnp.float32)
    inv_right = inv_out.astype(jnp.float32)

    def one_block(block):
        start = (block * QRY_DEV).astype(jnp.int32)
        query_part = lax.dynamic_slice_in_dim(queries, start, QRY_DEV, 0).astype(jnp.float32)
        query_part = query_part.reshape(QRY_DEV, MODULES, R, R)
        left = jnp.einsum("mab,qmbc->qmac", inv_left, query_part, precision=lax.Precision.HIGHEST)
        left = lax.optimization_barrier(left.astype(jnp.bfloat16)).astype(jnp.float32)
        ready = jnp.einsum("qmac,mcd->qmad", left, inv_right, precision=lax.Precision.HIGHEST)
        ready = ready.reshape(QRY_DEV, GD).astype(jnp.bfloat16)
        listed_rows = lax.dynamic_slice_in_dim(listed, (block * (QRY_DEV // QB)).astype(jnp.int32), QRY_DEV // QB, 0)
        results = []
        for window in range(3):
            source = ((block + window - 1 + N_EX) % N_EX).astype(jnp.int32)
            slab = lax.dynamic_slice_in_dim(store, (source * EX_DEV).astype(jnp.int32), EX_DEV, 0)
            part = lax.dot_general(ready, slab, (((1,), (1,)), ((), ())), preferred_element_type=jnp.float32)
            results.append(part * widen(listed_rows[:, window * SB:(window + 1) * SB]))
        return jnp.stack(results)

    every = lax.map(one_block, jnp.arange(N_EX, dtype=jnp.int32))
    return jnp.transpose(every, (1, 0, 2, 3)).reshape(3, QUERIES, EX_DEV)
```

```python
import functools

import jax
import jax.numpy as jnp
from jax import lax
from jax.experimental import pallas as pl
from jax.experimental.pallas import tpu as pltpu
from jax.sharding import PartitionSpec as P

MESH = pl.DeviceIdType.MESH
F32 = jnp.float32
BF16 = jnp.bfloat16
QB = 32
SUB = 64
SELF, PARTNER, CROSS = 0, 1, 2
GROUP = 8


def nt_dot(a, b):
    return lax.dot_general(a, b, (((1,), (1,)), ((), ())), preferred_element_type=F32)


def iota(shape, dim):
    return lax.broadcasted_iota(jnp.int32, shape, dim)


def one_hot(cond):
    return jnp.where(cond, 1.0, 0.0).astype(BF16)


def place(a, b):
    return jnp.dot(a, b, preferred_element_type=F32).astype(BF16)


def split_factor(matrix, side):
    half = side // 2
    row = iota((side, side), 0)
    col = iota((side, side), 1)
    rows = one_hot(col == 2 * (row % half) + row // half)
    straight = one_hot(row == 2 * (col % half) + col // half)
    swapped = one_hot(row == 2 * (col % half) + 1 - col // half)
    picked = place(rows, matrix)
    upper = place(picked, straight)
    lower = place(picked, swapped)
    return jnp.where(row < half, upper.astype(F32), lower.astype(F32)).astype(BF16)


def twice(matrix, side):
    wide = 2 * side
    rows = one_hot(iota((wide, side), 0) % side == iota((wide, side), 1))
    cols = one_hot(iota((side, wide), 0) == iota((side, wide), 1) % side)
    full = place(place(rows, matrix), cols)
    same = iota((wide, wide), 0) // side == iota((wide, wide), 1) // side
    return jnp.where(same, full.astype(F32), 0.0).astype(BF16)


def kernel(
    n_ex, n_x,
    q_hbm, in_ref, out_ref, s_hbm, listed_ref, o_ref,
    raw, vraw, vis, slab, part, hop, mine, last, left_w, right_w, spread, gather, mask,
    raw_sem, slab_sem, vraw_send, vraw_recv, send_sem, recv_sem, hop_send, hop_recv, last_send, last_recv,
):
    modules, side, _ = in_ref.shape
    pairs = side // 2
    wide = 2 * side
    n_chunk = raw.shape[0]
    b = lax.axis_index("ex")
    g = lax.axis_index("grp")
    yl = g // n_x
    x = lax.rem(g, n_x)
    par = lax.rem(b, 2)
    partner = b + 1 - 2 * par
    cross = lax.rem(b - 1 + 2 * par + n_ex, n_ex)
    other = (1 - yl) * n_x + x

    def order(t):
        d = 1 + t // 2
        rel = lax.rem(t, 2)
        to_x = lax.rem(x + d, n_x)
        to_y = lax.rem(yl + rel, 2)
        return d, rel, to_x, to_y * n_x + to_x

    peers = [(b, other), (partner, g), (partner, other), (cross, g), (cross, other)]
    peers += [(b, yl * n_x + lax.rem(x + d, n_x)) for d in range(1, n_x)]
    barrier = pltpu.get_barrier_semaphore()
    for peer in peers:
        pl.semaphore_signal(barrier, inc=1, device_id=peer, device_id_type=MESH)

    def load_raw(t):
        j = order(t)[3]
        return pltpu.make_async_copy(q_hbm.at[pl.ds(pl.multiple_of(j * QB, QB), QB)], raw.at[j], raw_sem.at[t])

    for t in range(n_chunk):
        load_raw(t).start()
    slab_copy = pltpu.make_async_copy(s_hbm, slab, slab_sem)
    slab_copy.start()

    pl.semaphore_wait(barrier, len(peers))

    first = order(0)[3]
    raw_out = pltpu.make_async_remote_copy(
        q_hbm.at[pl.ds(pl.multiple_of(first * QB, QB), QB)], vraw, vraw_send, vraw_recv,
        device_id=(cross, g), device_id_type=MESH)
    raw_out.start()

    for m in range(modules):
        left_w[m] = split_factor(in_ref[m], side)
        right_w[m] = twice(out_ref[m], side)
    rows_l = listed_ref.shape[0]
    row = jnp.sum(
        jnp.where(iota(listed_ref.shape, 0) == g, listed_ref[...].astype(F32), 0.0), axis=0, keepdims=True)
    widths = (listed_ref.shape[1], mask.shape[1])
    fan = one_hot(iota(widths, 1) // SUB == iota(widths, 0))
    mask[...] = jnp.dot(
        jnp.broadcast_to(row, listed_ref.shape).astype(BF16), fan, preferred_element_type=F32)

    low = (iota((pairs, GROUP * wide), 1) % wide) < side

    def precondition(src, dst):
        for m in range(modules):
            base = m * side * side
            for p in range(pairs):
                spread[pl.ds(p, QB, stride=pairs), :] = src[:, base + p * wide:base + (p + 1) * wide].astype(F32)
            for q in range(0, QB, GROUP):
                rows = spread[q * pairs:(q + GROUP) * pairs, :]
                turned = pltpu.roll(rows, side, 1).astype(BF16)
                rows = rows.astype(BF16)
                lay = lambda v: jnp.concatenate([v[i * pairs:(i + 1) * pairs] for i in range(GROUP)], axis=1)
                both = jnp.concatenate([lay(rows), lay(turned)], axis=0)
                left = jnp.dot(left_w[m], both, preferred_element_type=F32)
                left = jnp.where(low, left[:pairs], left[pairs:]).astype(BF16)
                stack = jnp.concatenate([left[:, i * wide:(i + 1) * wide] for i in range(GROUP)], axis=0)
                gather[q * pairs:(q + GROUP) * pairs, :] = jnp.dot(stack, right_w[m], preferred_element_type=F32)
            for p in range(pairs):
                dst[:, base + p * wide:base + (p + 1) * wide] = gather[pl.ds(p, QB, stride=pairs), :].astype(BF16)

    def to_partner(j):
        return pltpu.make_async_remote_copy(
            vis.at[SELF, j], vis.at[PARTNER, j], send_sem.at[0, j], recv_sem.at[0, j],
            device_id=(partner, g), device_id_type=MESH)

    def to_cross(j):
        return pltpu.make_async_remote_copy(
            vis.at[SELF, j], vis.at[CROSS, j], send_sem.at[1, j], recv_sem.at[1, j],
            device_id=(cross, g), device_id_type=MESH)

    def prepare(t, carry):
        j = order(t)[3]
        load_raw(t).wait()
        precondition(raw.at[j], vis.at[SELF, j])

        @pl.when(t > 0)
        def _():
            to_cross(j).start()

        to_partner(j).start()
        return carry

    lax.fori_loop(0, n_chunk, prepare, 0)
    slab_copy.wait()

    depth = slab.shape[1]
    step = 1024

    def to_hop(w, t):
        d, rel, to_x, j = order(t)
        return pltpu.make_async_remote_copy(
            part.at[w, t], hop.at[w, rel, n_x - 1 - d], hop_send.at[w, t], hop_recv.at[w, rel, n_x - 1 - d],
            device_id=(b, yl * n_x + to_x), device_id_type=MESH)

    def score(w, t):
        j = order(t)[3]

        def inner(k, acc):
            at = pl.ds(pl.multiple_of(k * step, step), step)
            return acc + nt_dot(vis[w, j, :, at], slab[:, at])

        part[w, t] = lax.fori_loop(0, depth // step, inner, jnp.zeros(part.shape[2:], F32))

        @pl.when(t < n_chunk - 2)
        def _():
            to_hop(w, t).start()

    def own(t, carry):
        score(SELF, t)
        return carry

    def near(t, carry):
        to_partner(order(t)[3]).wait_recv()
        score(PARTNER, t)
        return carry

    def far(t, carry):
        to_cross(order(t)[3]).wait_recv()
        score(CROSS, t)
        return carry

    owner = (b, partner, cross)

    def to_last(w, rel):
        return pltpu.make_async_remote_copy(
            mine.at[w, rel], last.at[w, rel], last_send.at[w, rel], last_recv.at[w, rel],
            device_id=(owner[w], g if rel == 0 else other), device_id_type=MESH)

    def gather_x(w, rel):
        for d in range(1, n_x):
            to_hop(w, 2 * (d - 1) + rel).wait_recv()
        total = part[w, n_chunk - 2 + rel]
        for d in range(n_x - 1):
            total = total + hop[w, rel, d]
        mine[w, rel] = total
        if not (w == SELF and rel == 0):
            to_last(w, rel).start()

    def finish(w):
        width = part.shape[3]
        to_last(w, 1).wait_recv()
        if w == SELF:
            total = mine[w, 0] + last[w, 1]
            o_ref[1] = total * mask[0:1, width:2 * width]
            return
        to_last(w, 0).wait_recv()
        total = last[w, 0] + last[w, 1]
        upper = par == (1 if w == CROSS else 0)

        @pl.when(upper)
        def _():
            o_ref[2] = total * mask[0:1, 2 * width:3 * width]

        @pl.when(jnp.logical_not(upper))
        def _():
            o_ref[0] = total * mask[0:1, 0:width]

    lax.fori_loop(0, n_chunk, own, 0)
    lax.fori_loop(0, n_chunk, near, 0)

    raw_out.wait_recv()
    precondition(vraw, vis.at[CROSS, first])
    score(CROSS, 0)
    lax.fori_loop(1, 3, far, 0)
    for w in (SELF, PARTNER):
        for rel in range(2):
            gather_x(w, rel)
    lax.fori_loop(3, 5, far, 0)
    finish(SELF)
    finish(PARTNER)
    lax.fori_loop(5, n_chunk - 1, far, 0)
    gather_x(CROSS, 0)
    far(n_chunk - 1, 0)
    gather_x(CROSS, 1)

    raw_out.wait_send()

    def drain(t, carry):
        j = order(t)[3]
        to_partner(j).wait_send()

        @pl.when(t > 0)
        def _():
            to_cross(j).wait_send()

        @pl.when(t < n_chunk - 2)
        def _():
            for w in range(3):
                to_hop(w, t).wait_send()

        return carry

    lax.fori_loop(0, n_chunk, drain, 0)
    finish(CROSS)
    for w in range(3):
        for rel in range(2):
            if not (w == SELF and rel == 0):
                to_last(w, rel).wait_send()


def solution(mesh):
    n_ex = mesh.shape["ex"]
    n_grp = mesh.shape["grp"]
    n_x = n_grp // 2

    def body(queries, inv_in, inv_out, store, listed):
        count, dims = queries.shape
        examples = store.shape[0]
        n_chunk = count // QB
        modules, side, _ = inv_in.shape
        tile = (QB, examples)
        vmem = pl.BlockSpec(memory_space=pltpu.VMEM)
        hbm = pl.BlockSpec(memory_space=pl.ANY)
        dma = pltpu.SemaphoreType.DMA
        return pl.pallas_call(
            functools.partial(kernel, n_ex, n_x),
            out_shape=jax.ShapeDtypeStruct((3,) + tile, F32),
            in_specs=[hbm, vmem, vmem, hbm, vmem],
            out_specs=vmem,
            scratch_shapes=[
                pltpu.VMEM((n_chunk, QB, dims), BF16),
                pltpu.VMEM((QB, dims), BF16),
                pltpu.VMEM((3, n_chunk, QB, dims), BF16),
                pltpu.VMEM((examples, dims), BF16),
                pltpu.VMEM((3, n_chunk) + tile, F32),
                pltpu.VMEM((3, 2, n_x - 1) + tile, F32),
                pltpu.VMEM((3, 2) + tile, F32),
                pltpu.VMEM((3, 2) + tile, F32),
                pltpu.VMEM((modules, side, side), BF16),
                pltpu.VMEM((modules, 2 * side, 2 * side), BF16),
                pltpu.VMEM((QB * side // 2, 2 * side), F32),
                pltpu.VMEM((QB * side // 2, 2 * side), F32),
                pltpu.VMEM((listed.shape[0], listed.shape[1] * SUB), F32),
                dma((n_chunk,)),
                dma,
                dma,
                dma,
                dma((2, n_chunk)),
                dma((2, n_chunk)),
                dma((3, n_chunk)),
                dma((3, 2, n_x - 1)),
                dma((3, 2)),
                dma((3, 2)),
            ],
            compiler_params=pltpu.CompilerParams(
                collective_id=0, has_side_effects=True, vmem_limit_bytes=60 * 2**20),
        )(queries, inv_in, inv_out, store, listed)

    in_specs = (
        P("ex", "grp"),
        P("grp", None, None),
        P("grp", None, None),
        P("ex", "grp"),
        P("ex", None),
    )
    out_specs = P(None, ("ex", "grp"), None)
    return jax.shard_map(body, mesh=mesh, in_specs=in_specs, out_specs=out_specs, check_vma=False)
```

```python
import functools

import jax
import jax.numpy as jnp
from jax import lax
from jax.experimental import pallas as pl
from jax.experimental.pallas import tpu as pltpu
from jax.sharding import PartitionSpec as P

MESH = pl.DeviceIdType.MESH
F32 = jnp.float32
BF16 = jnp.bfloat16
QB = 32
SUB = 64
SELF, PARTNER, CROSS = 0, 1, 2
GROUP = 8
PIECES = 4


def nt_dot(a, b):
    return lax.dot_general(a, b, (((1,), (1,)), ((), ())), preferred_element_type=F32)


def iota(shape, dim):
    return lax.broadcasted_iota(jnp.int32, shape, dim)


def one_hot(cond):
    return jnp.where(cond, 1.0, 0.0).astype(BF16)


def place(a, b):
    return jnp.dot(a, b, preferred_element_type=F32).astype(BF16)


def split_factor(matrix, side):
    half = side // 2
    row = iota((side, side), 0)
    col = iota((side, side), 1)
    rows = one_hot(col == 2 * (row % half) + row // half)
    straight = one_hot(row == 2 * (col % half) + col // half)
    swapped = one_hot(row == 2 * (col % half) + 1 - col // half)
    picked = place(rows, matrix)
    upper = place(picked, straight)
    lower = place(picked, swapped)
    return jnp.where(row < half, upper.astype(F32), lower.astype(F32)).astype(BF16)


def twice(matrix, side):
    wide = 2 * side
    rows = one_hot(iota((wide, side), 0) % side == iota((wide, side), 1))
    cols = one_hot(iota((side, wide), 0) == iota((side, wide), 1) % side)
    full = place(place(rows, matrix), cols)
    same = iota((wide, wide), 0) // side == iota((wide, wide), 1) // side
    return jnp.where(same, full.astype(F32), 0.0).astype(BF16)


def kernel(
    n_ex, n_x,
    q_hbm, in_ref, out_ref, s_hbm, listed_ref, o_ref,
    raw, vraw, vis, slab, part, hop, mine, last, left_w, right_w, spread, gather, mask,
    raw_sem, slab_sem, vraw_send, vraw_recv, near_send, near_recv, far_send, far_recv, hop_send, hop_recv, last_send, last_recv,
):
    modules, side, _ = in_ref.shape
    pairs = side // 2
    wide = 2 * side
    n_chunk = raw.shape[0] // QB
    depth = slab.shape[1]
    b = lax.axis_index("ex")
    g = lax.axis_index("grp")
    yl = g // n_x
    x = lax.rem(g, n_x)
    par = lax.rem(b, 2)
    partner = b + 1 - 2 * par
    cross = lax.rem(b - 1 + 2 * par + n_ex, n_ex)
    other = (1 - yl) * n_x + x

    def order(t):
        d = 1 + t // 2
        rel = lax.rem(t, 2)
        to_x = lax.rem(x + d, n_x)
        to_y = lax.rem(yl + rel, 2)
        return d, rel, to_x, to_y * n_x + to_x

    peers = [(b, other), (partner, g), (partner, other), (cross, g), (cross, other)]
    peers += [(b, yl * n_x + lax.rem(x + d, n_x)) for d in range(1, n_x)]
    barrier = pltpu.get_barrier_semaphore()
    for peer in peers:
        pl.semaphore_signal(barrier, inc=1, device_id=peer, device_id_type=MESH)

    def rows_of(t):
        return pl.ds(pl.multiple_of(order(t)[3] * QB, QB), QB)

    def load_raw(t):
        return pltpu.make_async_copy(q_hbm.at[rows_of(t)], raw.at[rows_of(t)], raw_sem.at[t])

    for t in range(n_chunk):
        load_raw(t).start()
    slab_copy = pltpu.make_async_copy(s_hbm, slab, slab_sem)
    slab_copy.start()

    pl.semaphore_wait(barrier, len(peers))

    raw_out = pltpu.make_async_remote_copy(
        q_hbm.at[rows_of(0)], vraw, vraw_send, vraw_recv,
        device_id=(cross, g), device_id_type=MESH)
    raw_out.start()

    for m in range(modules):
        left_w[m] = split_factor(in_ref[m], side)
        right_w[m] = twice(out_ref[m], side)
    rows_l = listed_ref.shape[0]
    row = jnp.sum(
        jnp.where(iota(listed_ref.shape, 0) == g, listed_ref[...].astype(F32), 0.0), axis=0, keepdims=True)
    widths = (listed_ref.shape[1], mask.shape[1])
    fan = one_hot(iota(widths, 1) // SUB == iota(widths, 0))
    mask[...] = jnp.dot(
        jnp.broadcast_to(row, listed_ref.shape).astype(BF16), fan, preferred_element_type=F32)

    low = (iota((pairs, GROUP * wide), 1) % wide) < side

    def precondition(src, dst):
        for m in range(modules):
            base = m * side * side
            for p in range(pairs):
                spread[pl.ds(p, QB, stride=pairs), :] = src[:, base + p * wide:base + (p + 1) * wide].astype(F32)
            for q in range(0, QB, GROUP):
                rows = spread[q * pairs:(q + GROUP) * pairs, :]
                turned = pltpu.roll(rows, side, 1).astype(BF16)
                rows = rows.astype(BF16)
                lay = lambda v: jnp.concatenate([v[i * pairs:(i + 1) * pairs] for i in range(GROUP)], axis=1)
                both = jnp.concatenate([lay(rows), lay(turned)], axis=0)
                left = jnp.dot(left_w[m], both, preferred_element_type=F32)
                left = jnp.where(low, left[:pairs], left[pairs:]).astype(BF16)
                stack = jnp.concatenate([left[:, i * wide:(i + 1) * wide] for i in range(GROUP)], axis=0)
                gather[q * pairs:(q + GROUP) * pairs, :] = jnp.dot(stack, right_w[m], preferred_element_type=F32)
            for p in range(pairs):
                dst[:, base + p * wide:base + (p + 1) * wide] = gather[pl.ds(p, QB, stride=pairs), :].astype(BF16)

    piece = depth // PIECES

    def to_partner(t):
        return pltpu.make_async_remote_copy(
            vis.at[SELF, rows_of(t)], vis.at[PARTNER, rows_of(t)], near_send.at[t], near_recv.at[t],
            device_id=(partner, g), device_id_type=MESH)

    def columns(k):
        return pl.ds(pl.multiple_of(k * piece, piece), piece)

    def to_cross(t, k):
        return pltpu.make_async_remote_copy(
            vis.at[SELF, rows_of(t), columns(k)], vis.at[CROSS, rows_of(t), columns(k)],
            far_send.at[t, k], far_recv.at[t, k], device_id=(cross, g), device_id_type=MESH)

    def prepare(t, carry):
        load_raw(t).wait()
        precondition(raw.at[rows_of(t)], vis.at[SELF, rows_of(t)])

        @pl.when(t > 0)
        def _():
            for k in range(PIECES):
                to_cross(t, k).start()

        to_partner(t).start()
        return carry

    lax.fori_loop(0, n_chunk, prepare, 0)
    slab_copy.wait()

    def to_hop(w, t):
        d, rel, to_x, j = order(t)
        return pltpu.make_async_remote_copy(
            part.at[w, rows_of(t)], hop.at[w, rel, n_x - 1 - d], hop_send.at[w, t], hop_recv.at[w, rel, n_x - 1 - d],
            device_id=(b, yl * n_x + to_x), device_id_type=MESH)

    def score_all(w):
        part[w] = nt_dot(vis[w, :, 0:piece], slab[:, 0:piece])

        def inner(k, carry):
            part[w] += nt_dot(vis[w, :, columns(k)], slab[:, columns(k)])
            return carry

        lax.fori_loop(1, PIECES, inner, 0)

        def send(t, carry):
            to_hop(w, t).start()
            return carry

        lax.fori_loop(0, n_chunk - 2, send, 0)

    def far(t, arrives):
        rows = rows_of(t)

        def inner(k, acc):
            if arrives:
                to_cross(t, k).wait_recv()
            return acc + nt_dot(vis[CROSS, rows, columns(k)], slab[:, columns(k)])

        part[CROSS, rows] = lax.fori_loop(0, PIECES, inner, jnp.zeros((QB, part.shape[2]), F32))

        @pl.when(t < n_chunk - 2)
        def _():
            to_hop(CROSS, t).start()

    def far_step(t, carry):
        far(t, True)
        return carry

    owner = (b, partner, cross)

    def to_last(w, rel):
        return pltpu.make_async_remote_copy(
            mine.at[w, rel], last.at[w, rel], last_send.at[w, rel], last_recv.at[w, rel],
            device_id=(owner[w], g if rel == 0 else other), device_id_type=MESH)

    def gather_x(w, rel):
        for d in range(1, n_x):
            to_hop(w, 2 * (d - 1) + rel).wait_recv()
        total = part[w, rows_of(n_chunk - 2 + rel)]
        for d in range(n_x - 1):
            total = total + hop[w, rel, d]
        mine[w, rel] = total
        if not (w == SELF and rel == 0):
            to_last(w, rel).start()

    def finish(w):
        width = part.shape[2]
        to_last(w, 1).wait_recv()
        if w == SELF:
            total = mine[w, 0] + last[w, 1]
            o_ref[1] = total * mask[0:1, width:2 * width]
            return
        to_last(w, 0).wait_recv()
        total = last[w, 0] + last[w, 1]
        upper = par == (1 if w == CROSS else 0)

        @pl.when(upper)
        def _():
            o_ref[2] = total * mask[0:1, 2 * width:3 * width]

        @pl.when(jnp.logical_not(upper))
        def _():
            o_ref[0] = total * mask[0:1, 0:width]

    score_all(SELF)
    for t in range(n_chunk):
        to_partner(t).wait_recv()
    score_all(PARTNER)

    for w in (SELF, PARTNER):
        for rel in range(2):
            gather_x(w, rel)

    raw_out.wait_recv()
    precondition(vraw, vis.at[CROSS, rows_of(0)])
    far(0, False)
    lax.fori_loop(1, n_chunk - 1, far_step, 0)
    gather_x(CROSS, 0)
    far(n_chunk - 1, True)
    gather_x(CROSS, 1)
    finish(SELF)
    finish(PARTNER)

    raw_out.wait_send()

    def drain(t, carry):
        to_partner(t).wait_send()

        @pl.when(t > 0)
        def _():
            for k in range(PIECES):
                to_cross(t, k).wait_send()

        @pl.when(t < n_chunk - 2)
        def _():
            for w in range(3):
                to_hop(w, t).wait_send()

        return carry

    lax.fori_loop(0, n_chunk, drain, 0)
    finish(CROSS)
    for w in range(3):
        for rel in range(2):
            if not (w == SELF and rel == 0):
                to_last(w, rel).wait_send()


def solution(mesh):
    n_ex = mesh.shape["ex"]
    n_grp = mesh.shape["grp"]
    n_x = n_grp // 2

    def body(queries, inv_in, inv_out, store, listed):
        count, dims = queries.shape
        examples = store.shape[0]
        n_chunk = count // QB
        modules, side, _ = inv_in.shape
        tile = (QB, examples)
        vmem = pl.BlockSpec(memory_space=pltpu.VMEM)
        hbm = pl.BlockSpec(memory_space=pl.ANY)
        dma = pltpu.SemaphoreType.DMA
        return pl.pallas_call(
            functools.partial(kernel, n_ex, n_x),
            out_shape=jax.ShapeDtypeStruct((3,) + tile, F32),
            in_specs=[hbm, vmem, vmem, hbm, vmem],
            out_specs=vmem,
            scratch_shapes=[
                pltpu.VMEM((count, dims), BF16),
                pltpu.VMEM((QB, dims), BF16),
                pltpu.VMEM((3, count, dims), BF16),
                pltpu.VMEM((examples, dims), BF16),
                pltpu.VMEM((3, count, examples), F32),
                pltpu.VMEM((3, 2, n_x - 1) + tile, F32),
                pltpu.VMEM((3, 2) + tile, F32),
                pltpu.VMEM((3, 2) + tile, F32),
                pltpu.VMEM((modules, side, side), BF16),
                pltpu.VMEM((modules, 2 * side, 2 * side), BF16),
                pltpu.VMEM((QB * side // 2, 2 * side), F32),
                pltpu.VMEM((QB * side // 2, 2 * side), F32),
                pltpu.VMEM((listed.shape[0], listed.shape[1] * SUB), F32),
                dma((n_chunk,)),
                dma,
                dma,
                dma,
                dma((n_chunk,)),
                dma((n_chunk,)),
                dma((n_chunk, PIECES)),
                dma((n_chunk, PIECES)),
                dma((3, n_chunk)),
                dma((3, 2, n_x - 1)),
                dma((3, 2)),
                dma((3, 2)),
            ],
            compiler_params=pltpu.CompilerParams(
                collective_id=0, has_side_effects=True, vmem_limit_bytes=60 * 2**20),
        )(queries, inv_in, inv_out, store, listed)

    in_specs = (
        P("ex", "grp"),
        P("grp", None, None),
        P("grp", None, None),
        P("ex", "grp"),
        P("ex", None),
    )
    out_specs = P(None, ("ex", "grp"), None)
    return jax.shard_map(body, mesh=mesh, in_specs=in_specs, out_specs=out_specs, check_vma=False)
```

```python
import functools

import jax
import jax.numpy as jnp
from jax import lax
from jax.experimental import pallas as pl
from jax.experimental.pallas import tpu as pltpu
from jax.sharding import PartitionSpec as P

MESH = pl.DeviceIdType.MESH
F32 = jnp.float32
BF16 = jnp.bfloat16
QB = 32
SUB = 64
SELF, PARTNER, CROSS = 0, 1, 2
GROUP = 8
PIECES = 8


def nt_dot(a, b):
    return lax.dot_general(a, b, (((1,), (1,)), ((), ())), preferred_element_type=F32)


def iota(shape, dim):
    return lax.broadcasted_iota(jnp.int32, shape, dim)


def one_hot(cond):
    return jnp.where(cond, 1.0, 0.0).astype(BF16)


def place(a, b):
    return jnp.dot(a, b, preferred_element_type=F32).astype(BF16)


def split_factor(matrix, side):
    half = side // 2
    row = iota((side, side), 0)
    col = iota((side, side), 1)
    rows = one_hot(col == 2 * (row % half) + row // half)
    straight = one_hot(row == 2 * (col % half) + col // half)
    swapped = one_hot(row == 2 * (col % half) + 1 - col // half)
    picked = place(rows, matrix)
    upper = place(picked, straight)
    lower = place(picked, swapped)
    return jnp.where(row < half, upper.astype(F32), lower.astype(F32)).astype(BF16)


def twice(matrix, side):
    wide = 2 * side
    rows = one_hot(iota((wide, side), 0) % side == iota((wide, side), 1))
    cols = one_hot(iota((side, wide), 0) == iota((side, wide), 1) % side)
    full = place(place(rows, matrix), cols)
    same = iota((wide, wide), 0) // side == iota((wide, wide), 1) // side
    return jnp.where(same, full.astype(F32), 0.0).astype(BF16)


def kernel(
    n_ex, n_x,
    q_hbm, in_hbm, out_hbm, s_hbm, listed_hbm, o_ref,
    in_ref, out_ref, listed_ref, raw, vraw, vis, slab, part, hop, mine, last, left_w, right_w, spread, gather, mask,
    small_sem, raw_sem, slab_sem, vraw_send, vraw_recv, near_send, near_recv, far_send, far_recv, hop_send, hop_recv, last_send, last_recv,
):
    modules, side, _ = in_ref.shape
    pairs = side // 2
    wide = 2 * side
    n_chunk = raw.shape[0] // QB
    depth = slab.shape[1]
    b = lax.axis_index("ex")
    g = lax.axis_index("grp")
    yl = g // n_x
    x = lax.rem(g, n_x)
    par = lax.rem(b, 2)
    partner = b + 1 - 2 * par
    cross = lax.rem(b - 1 + 2 * par + n_ex, n_ex)
    other = (1 - yl) * n_x + x

    def order(t):
        d = 1 + t // 2
        rel = lax.rem(t, 2)
        to_x = lax.rem(x + d, n_x)
        to_y = lax.rem(yl + rel, 2)
        return d, rel, to_x, to_y * n_x + to_x

    peers = [(b, other), (partner, g), (partner, other), (cross, g), (cross, other)]
    peers += [(b, yl * n_x + lax.rem(x + d, n_x)) for d in range(1, n_x)]
    barrier = pltpu.get_barrier_semaphore()
    for peer in peers:
        pl.semaphore_signal(barrier, inc=1, device_id=peer, device_id_type=MESH)

    def rows_of(t):
        return pl.ds(pl.multiple_of(order(t)[3] * QB, QB), QB)

    def load_raw(t):
        return pltpu.make_async_copy(q_hbm.at[rows_of(t)], raw.at[rows_of(t)], raw_sem.at[t])

    small = [
        pltpu.make_async_copy(source, target, small_sem.at[i])
        for i, (source, target) in enumerate([(in_hbm, in_ref), (out_hbm, out_ref), (listed_hbm, listed_ref)])
    ]
    for copy in small:
        copy.start()
    for t in range(n_chunk):
        load_raw(t).start()
    slab_copy = pltpu.make_async_copy(s_hbm, slab, slab_sem)
    slab_copy.start()

    pl.semaphore_wait(barrier, len(peers))

    raw_out = pltpu.make_async_remote_copy(
        q_hbm.at[rows_of(0)], vraw, vraw_send, vraw_recv,
        device_id=(cross, g), device_id_type=MESH)
    raw_out.start()

    for copy in small:
        copy.wait()
    for m in range(modules):
        left_w[m] = split_factor(in_ref[m], side)
        right_w[m] = twice(out_ref[m], side)
    row = jnp.sum(
        jnp.where(iota(listed_ref.shape, 0) == g, listed_ref[...].astype(F32), 0.0), axis=0, keepdims=True)
    widths = (listed_ref.shape[1], mask.shape[1])
    fan = one_hot(iota(widths, 1) // SUB == iota(widths, 0))
    mask[...] = jnp.dot(
        jnp.broadcast_to(row, listed_ref.shape).astype(BF16), fan, preferred_element_type=F32)

    low = (iota((pairs, GROUP * wide), 1) % wide) < side

    def precondition(src, dst):
        for m in range(modules):
            base = m * side * side
            for p in range(pairs):
                spread[pl.ds(p, QB, stride=pairs), :] = src[:, base + p * wide:base + (p + 1) * wide].astype(F32)
            for q in range(0, QB, GROUP):
                rows = spread[q * pairs:(q + GROUP) * pairs, :]
                turned = pltpu.roll(rows, side, 1).astype(BF16)
                rows = rows.astype(BF16)
                lay = lambda v: jnp.concatenate([v[i * pairs:(i + 1) * pairs] for i in range(GROUP)], axis=1)
                both = jnp.concatenate([lay(rows), lay(turned)], axis=0)
                left = jnp.dot(left_w[m], both, preferred_element_type=F32)
                left = jnp.where(low, left[:pairs], left[pairs:]).astype(BF16)
                stack = jnp.concatenate([left[:, i * wide:(i + 1) * wide] for i in range(GROUP)], axis=0)
                gather[q * pairs:(q + GROUP) * pairs, :] = jnp.dot(stack, right_w[m], preferred_element_type=F32)
            for p in range(pairs):
                dst[:, base + p * wide:base + (p + 1) * wide] = gather[pl.ds(p, QB, stride=pairs), :].astype(BF16)

    piece = depth // PIECES

    def to_partner(t):
        return pltpu.make_async_remote_copy(
            vis.at[SELF, rows_of(t)], vis.at[PARTNER, rows_of(t)], near_send.at[t], near_recv.at[t],
            device_id=(partner, g), device_id_type=MESH)

    def columns(k):
        return pl.ds(pl.multiple_of(k * piece, piece), piece)

    def to_cross(t, k):
        return pltpu.make_async_remote_copy(
            vis.at[SELF, rows_of(t), columns(k)], vis.at[CROSS, rows_of(t), columns(k)],
            far_send.at[t, k], far_recv.at[t, k], device_id=(cross, g), device_id_type=MESH)

    def prepare(t, carry):
        load_raw(t).wait()
        precondition(raw.at[rows_of(t)], vis.at[SELF, rows_of(t)])

        @pl.when(t > 0)
        def _():
            for k in range(PIECES):
                to_cross(t, k).start()

        to_partner(t).start()
        return carry

    lax.fori_loop(0, n_chunk, prepare, 0)
    slab_copy.wait()

    def to_hop(w, t):
        d, rel, to_x, j = order(t)
        return pltpu.make_async_remote_copy(
            part.at[w, rows_of(t)], hop.at[w, rel, n_x - 1 - d], hop_send.at[w, t], hop_recv.at[w, rel, n_x - 1 - d],
            device_id=(b, yl * n_x + to_x), device_id_type=MESH)

    def score_all(w):
        part[w] = nt_dot(vis[w, :, 0:piece], slab[:, 0:piece])

        def inner(k, carry):
            part[w] += nt_dot(vis[w, :, columns(k)], slab[:, columns(k)])
            return carry

        lax.fori_loop(1, PIECES, inner, 0)

        def send(t, carry):
            to_hop(w, t).start()
            return carry

        lax.fori_loop(0, n_chunk - 2, send, 0)

    def far(t, arrives):
        rows = rows_of(t)

        def inner(k, acc):
            if arrives:
                to_cross(t, k).wait_recv()
            return acc + nt_dot(vis[CROSS, rows, columns(k)], slab[:, columns(k)])

        part[CROSS, rows] = lax.fori_loop(0, PIECES, inner, jnp.zeros((QB, part.shape[2]), F32))

        @pl.when(t < n_chunk - 2)
        def _():
            to_hop(CROSS, t).start()

    def far_step(t, carry):
        far(t, True)
        return carry

    owner = (b, partner, cross)

    def to_last(w, rel):
        return pltpu.make_async_remote_copy(
            mine.at[w, rel], last.at[w, rel], last_send.at[w, rel], last_recv.at[w, rel],
            device_id=(owner[w], g if rel == 0 else other), device_id_type=MESH)

    def gather_x(w, rel):
        for d in range(1, n_x):
            to_hop(w, 2 * (d - 1) + rel).wait_recv()
        total = part[w, rows_of(n_chunk - 2 + rel)]
        for d in range(n_x - 1):
            total = total + hop[w, rel, d]
        mine[w, rel] = total.astype(mine.dtype)
        if not (w == SELF and rel == 0):
            to_last(w, rel).start()

    def finish(w):
        width = part.shape[2]
        to_last(w, 1).wait_recv()
        if w == SELF:
            total = mine[w, 0].astype(F32) + last[w, 1].astype(F32)
            o_ref[1] = total * mask[0:1, width:2 * width]
            return
        to_last(w, 0).wait_recv()
        total = last[w, 0].astype(F32) + last[w, 1].astype(F32)
        upper = par == (1 if w == CROSS else 0)

        @pl.when(upper)
        def _():
            o_ref[2] = total * mask[0:1, 2 * width:3 * width]

        @pl.when(jnp.logical_not(upper))
        def _():
            o_ref[0] = total * mask[0:1, 0:width]

    score_all(SELF)
    for t in range(n_chunk):
        to_partner(t).wait_recv()
    score_all(PARTNER)

    for w in (SELF, PARTNER):
        for rel in range(2):
            gather_x(w, rel)

    raw_out.wait_recv()
    precondition(vraw, vis.at[CROSS, rows_of(0)])
    far(0, False)
    lax.fori_loop(1, n_chunk - 1, far_step, 0)
    gather_x(CROSS, 0)
    far(n_chunk - 1, True)
    gather_x(CROSS, 1)
    finish(SELF)
    finish(PARTNER)

    raw_out.wait_send()

    def drain(t, carry):
        to_partner(t).wait_send()

        @pl.when(t > 0)
        def _():
            for k in range(PIECES):
                to_cross(t, k).wait_send()

        @pl.when(t < n_chunk - 2)
        def _():
            for w in range(3):
                to_hop(w, t).wait_send()

        return carry

    lax.fori_loop(0, n_chunk, drain, 0)
    finish(CROSS)
    for w in range(3):
        for rel in range(2):
            if not (w == SELF and rel == 0):
                to_last(w, rel).wait_send()


def solution(mesh):
    n_ex = mesh.shape["ex"]
    n_grp = mesh.shape["grp"]
    n_x = n_grp // 2

    def body(queries, inv_in, inv_out, store, listed):
        count, dims = queries.shape
        examples = store.shape[0]
        n_chunk = count // QB
        modules, side, _ = inv_in.shape
        tile = (QB, examples)
        vmem = pl.BlockSpec(memory_space=pltpu.VMEM)
        hbm = pl.BlockSpec(memory_space=pltpu.HBM)
        dma = pltpu.SemaphoreType.DMA
        return pl.pallas_call(
            functools.partial(kernel, n_ex, n_x),
            out_shape=jax.ShapeDtypeStruct((3,) + tile, F32),
            in_specs=[hbm] * 5,
            out_specs=vmem,
            scratch_shapes=[
                pltpu.VMEM(inv_in.shape, BF16),
                pltpu.VMEM(inv_out.shape, BF16),
                pltpu.VMEM(listed.shape, listed.dtype),
                pltpu.VMEM((count, dims), BF16),
                pltpu.VMEM((QB, dims), BF16),
                pltpu.VMEM((3, count, dims), BF16),
                pltpu.VMEM((examples, dims), BF16),
                pltpu.VMEM((3, count, examples), F32),
                pltpu.VMEM((3, 2, n_x - 1) + tile, F32),
                pltpu.VMEM((3, 2) + tile, BF16),
                pltpu.VMEM((3, 2) + tile, BF16),
                pltpu.VMEM((modules, side, side), BF16),
                pltpu.VMEM((modules, 2 * side, 2 * side), BF16),
                pltpu.VMEM((QB * side // 2, 2 * side), F32),
                pltpu.VMEM((QB * side // 2, 2 * side), F32),
                pltpu.VMEM((listed.shape[0], listed.shape[1] * SUB), F32),
                dma((3,)),
                dma((n_chunk,)),
                dma,
                dma,
                dma,
                dma((n_chunk,)),
                dma((n_chunk,)),
                dma((n_chunk, PIECES)),
                dma((n_chunk, PIECES)),
                dma((3, n_chunk)),
                dma((3, 2, n_x - 1)),
                dma((3, 2)),
                dma((3, 2)),
            ],
            compiler_params=pltpu.CompilerParams(
                collective_id=0, has_side_effects=True, vmem_limit_bytes=36 * 2**20),
        )(*[pltpu.with_memory_space_constraint(v, pltpu.HBM) for v in (queries, inv_in, inv_out, store, listed)])

    in_specs = (
        P("ex", "grp"),
        P("grp", None, None),
        P("grp", None, None),
        P("ex", "grp"),
        P("ex", None),
    )
    out_specs = P(None, ("ex", "grp"), None)
    return jax.shard_map(body, mesh=mesh, in_specs=in_specs, out_specs=out_specs, check_vma=False)
```

```python
import functools

import jax
import jax.numpy as jnp
from jax import lax
from jax.experimental import pallas as pl
from jax.experimental.pallas import tpu as pltpu
from jax.sharding import PartitionSpec as P

MESH = pl.DeviceIdType.MESH
F32 = jnp.float32
BF16 = jnp.bfloat16
QB = 32
SUB = 64
SELF, PARTNER, CROSS = 0, 1, 2
GROUP = 8
PIECES = (2, 4, 8, 16, 16)
SPAN = 4096


def nt_dot(a, b):
    return lax.dot_general(a, b, (((1,), (1,)), ((), ())), preferred_element_type=F32)


def iota(shape, dim):
    return lax.broadcasted_iota(jnp.int32, shape, dim)


def one_hot(cond):
    return jnp.where(cond, 1.0, 0.0).astype(BF16)


def place(a, b):
    return jnp.dot(a, b, preferred_element_type=F32).astype(BF16)


def split_factor(matrix, side):
    half = side // 2
    row = iota((side, side), 0)
    col = iota((side, side), 1)
    rows = one_hot(col == 2 * (row % half) + row // half)
    straight = one_hot(row == 2 * (col % half) + col // half)
    swapped = one_hot(row == 2 * (col % half) + 1 - col // half)
    picked = place(rows, matrix)
    upper = place(picked, straight)
    lower = place(picked, swapped)
    return jnp.where(row < half, upper.astype(F32), lower.astype(F32)).astype(BF16)


def twice(matrix, side):
    wide = 2 * side
    rows = one_hot(iota((wide, side), 0) % side == iota((wide, side), 1))
    cols = one_hot(iota((side, wide), 0) == iota((side, wide), 1) % side)
    full = place(place(rows, matrix), cols)
    same = iota((wide, wide), 0) // side == iota((wide, wide), 1) // side
    return jnp.where(same, full.astype(F32), 0.0).astype(BF16)


def kernel(
    n_ex, n_x,
    q_hbm, in_hbm, out_hbm, s_hbm, listed_hbm, o_ref,
    in_ref, out_ref, listed_ref, raw, vraw, vis, slab, part, hop, mine, last, left_w, right_w, spread, gather, mask,
    small_sem, raw_sem, slab_sem, vraw_send, vraw_recv, near_send, near_recv, far_send, far_recv, tail_recv, hop_send, hop_recv, last_send, last_recv,
):
    modules, side, _ = in_ref.shape
    pairs = side // 2
    wide = 2 * side
    n_chunk = raw.shape[0] // QB
    depth = slab.shape[1]
    b = lax.axis_index("ex")
    g = lax.axis_index("grp")
    yl = g // n_x
    x = lax.rem(g, n_x)
    par = lax.rem(b, 2)
    partner = b + 1 - 2 * par
    cross = lax.rem(b - 1 + 2 * par + n_ex, n_ex)
    other = (1 - yl) * n_x + x

    def order(t):
        d = 1 + t // 2
        rel = lax.rem(t, 2)
        to_x = lax.rem(x + d, n_x)
        to_y = lax.rem(yl + rel, 2)
        return d, rel, to_x, to_y * n_x + to_x

    peers = [(b, other), (partner, g), (partner, other), (cross, g), (cross, other)]
    peers += [(b, yl * n_x + lax.rem(x + d, n_x)) for d in range(1, n_x)]
    barrier = pltpu.get_barrier_semaphore()
    for peer in peers:
        pl.semaphore_signal(barrier, inc=1, device_id=peer, device_id_type=MESH)

    def rows_of(t):
        return pl.ds(pl.multiple_of(order(t)[3] * QB, QB), QB)

    def load_raw(t):
        return pltpu.make_async_copy(q_hbm.at[rows_of(t)], raw.at[rows_of(t)], raw_sem.at[t])

    small = [
        pltpu.make_async_copy(source, target, small_sem.at[i])
        for i, (source, target) in enumerate([(in_hbm, in_ref), (out_hbm, out_ref), (listed_hbm, listed_ref)])
    ]
    for copy in small:
        copy.start()
    for i in range(n_chunk):
        load_raw((i + 1) % n_chunk).start()
    slab_copy = pltpu.make_async_copy(s_hbm, slab, slab_sem)
    slab_copy.start()

    pl.semaphore_wait(barrier, len(peers))

    raw_out = pltpu.make_async_remote_copy(
        q_hbm.at[rows_of(0)], vraw, vraw_send, vraw_recv,
        device_id=(cross, g), device_id_type=MESH)
    raw_out.start()

    for copy in small:
        copy.wait()
    for m in range(modules):
        left_w[m] = split_factor(in_ref[m], side)
        right_w[m] = twice(out_ref[m], side)
    row = jnp.sum(
        jnp.where(iota(listed_ref.shape, 0) == g, listed_ref[...].astype(F32), 0.0), axis=0, keepdims=True)
    fan_shape = (listed_ref.shape[1], mask.shape[1])
    fan = one_hot(iota(fan_shape, 1) // SUB == iota(fan_shape, 0))
    mask[...] = jnp.dot(
        jnp.broadcast_to(row, listed_ref.shape).astype(BF16), fan, preferred_element_type=F32)

    low = (iota((pairs, GROUP * wide), 1) % wide) < side

    def precondition(src, dst):
        for m in range(modules):
            base = m * side * side
            for p in range(pairs):
                spread[pl.ds(p, QB, stride=pairs), :] = src[:, base + p * wide:base + (p + 1) * wide].astype(F32)
            for q in range(0, QB, GROUP):
                rows = spread[q * pairs:(q + GROUP) * pairs, :]
                turned = pltpu.roll(rows, side, 1).astype(BF16)
                rows = rows.astype(BF16)
                lay = lambda v: jnp.concatenate([v[i * pairs:(i + 1) * pairs] for i in range(GROUP)], axis=1)
                both = jnp.concatenate([lay(rows), lay(turned)], axis=0)
                left = jnp.dot(left_w[m], both, preferred_element_type=F32)
                left = jnp.where(low, left[:pairs], left[pairs:]).astype(BF16)
                stack = jnp.concatenate([left[:, i * wide:(i + 1) * wide] for i in range(GROUP)], axis=0)
                gather[q * pairs:(q + GROUP) * pairs, :] = jnp.dot(stack, right_w[m], preferred_element_type=F32)
            for p in range(pairs):
                dst[:, base + p * wide:base + (p + 1) * wide] = gather[pl.ds(p, QB, stride=pairs), :].astype(BF16)

    def to_partner(rows):
        return pltpu.make_async_remote_copy(
            vis.at[SELF, rows], vis.at[PARTNER, rows], near_send, near_recv,
            device_id=(partner, g), device_id_type=MESH)

    def to_cross(t):
        return pltpu.make_async_remote_copy(
            vis.at[SELF, rows_of(t)], vis.at[CROSS, rows_of(t)], far_send, far_recv.at[t],
            device_id=(cross, g), device_id_type=MESH)

    widths = [depth // fraction for fraction in PIECES]
    cuts = [slice(sum(widths[:k]), sum(widths[:k + 1])) for k in range(len(widths))]

    def tail_piece(k):
        at = rows_of(n_chunk - 1), cuts[k]
        return pltpu.make_async_remote_copy(
            vis.at[(SELF,) + at], vis.at[(CROSS,) + at], far_send, tail_recv.at[k],
            device_id=(cross, g), device_id_type=MESH)

    def prepare(i, carry):
        t = lax.rem(i + 1, n_chunk)
        load_raw(t).wait()
        precondition(raw.at[rows_of(t)], vis.at[SELF, rows_of(t)])

        @pl.when(jnp.logical_and(t > 0, t < n_chunk - 1))
        def _():
            to_cross(t).start()

        @pl.when(t == n_chunk - 1)
        def _():
            for k in range(len(cuts)):
                tail_piece(k).start()

        to_partner(rows_of(t)).start()
        return carry

    lax.fori_loop(0, n_chunk, prepare, 0)
    slab_copy.wait()

    def to_hop(w, t):
        d, rel, to_x, j = order(t)
        return pltpu.make_async_remote_copy(
            part.at[w, rows_of(t)], hop.at[w, rel, n_x - 1 - d], hop_send.at[w], hop_recv.at[w, rel],
            device_id=(b, yl * n_x + to_x), device_id_type=MESH)

    spans = [slice(at, at + SPAN) for at in range(0, depth, SPAN)]

    def score_all(w):
        for at in spans:
            product = nt_dot(vis[w, :, at], slab[:, at])
            part[w] = product if at.start == 0 else part[w] + product

        def send(t, carry):
            to_hop(w, t).start()
            return carry

        lax.fori_loop(0, n_chunk - 2, send, 0)

    def far(t):
        rows = rows_of(t)
        part[CROSS, rows] = sum(nt_dot(vis[CROSS, rows, at], slab[:, at]) for at in spans)

    def far_pieces(t):
        rows = rows_of(t)
        total = 0.0
        for k, at in enumerate(cuts):
            tail_piece(k).wait_recv()
            total += nt_dot(vis[CROSS, rows, at], slab[:, at])
        part[CROSS, rows] = total

    def far_step(t, carry):
        @pl.when(t > 0)
        def _():
            to_cross(t).wait_recv()

        far(t)

        @pl.when(t < n_chunk - 2)
        def _():
            to_hop(CROSS, t).start()

        return carry

    owner = (b, partner, cross)

    def to_last(w, rel):
        return pltpu.make_async_remote_copy(
            mine.at[w, rel], last.at[w, rel], last_send.at[min(w, 1)], last_recv.at[w],
            device_id=(owner[w], g if rel == 0 else other), device_id_type=MESH)

    def group(ref, send, recv):
        return pltpu.make_async_remote_copy(
            ref, ref, send, recv, device_id=(partner, g), device_id_type=MESH)

    def gather_x(w, rel):
        group(hop.at[w, rel], hop_send.at[w], hop_recv.at[w, rel]).wait_recv()
        rows = rows_of(n_chunk - 2 + rel)
        total = part[w, rows]
        for d in range(n_x - 1):
            total = total + hop[w, rel, d]
        if w == SELF and rel == 0:
            part[w, rows] = total
        else:
            mine[w, rel] = total.astype(mine.dtype)
            to_last(w, rel).start()

    def finish(w):
        width = part.shape[2]
        if w == SELF:
            to_last(w, 1).wait_recv()
            total = part[w, rows_of(n_chunk - 2)] + last[w, 1].astype(F32)
            o_ref[1] = total * mask[0:1, width:2 * width]
            return
        group(last.at[w], last_send.at[1], last_recv.at[w]).wait_recv()
        total = last[w, 0].astype(F32) + last[w, 1].astype(F32)
        upper = par == (1 if w == CROSS else 0)

        @pl.when(upper)
        def _():
            o_ref[2] = total * mask[0:1, 2 * width:3 * width]

        @pl.when(jnp.logical_not(upper))
        def _():
            o_ref[0] = total * mask[0:1, 0:width]

    score_all(SELF)
    to_partner(slice(None)).wait_recv()
    score_all(PARTNER)

    for w in (SELF, PARTNER):
        for rel in range(2):
            gather_x(w, rel)

    raw_out.wait_recv()
    precondition(vraw, vis.at[CROSS, rows_of(0)])
    lax.fori_loop(0, n_chunk - 1, far_step, 0)
    gather_x(CROSS, 0)
    far_pieces(n_chunk - 1)
    gather_x(CROSS, 1)
    finish(SELF)
    finish(PARTNER)

    raw_out.wait_send()
    to_partner(slice(None)).wait_send()
    group(vis.at[SELF, 0:(n_chunk - 1) * QB], far_send, far_recv.at[0]).wait_send()
    for w in range(3):
        group(part.at[w, 0:(n_chunk - 2) * QB], hop_send.at[w], hop_recv.at[w, 0]).wait_send()
    to_last(SELF, 1).wait_send()
    group(mine.at[1:3], last_send.at[1], last_recv.at[1]).wait_send()
    finish(CROSS)


def solution(mesh):
    n_ex = mesh.shape["ex"]
    n_grp = mesh.shape["grp"]
    n_x = n_grp // 2

    def body(queries, inv_in, inv_out, store, listed):
        count, dims = queries.shape
        examples = store.shape[0]
        n_chunk = count // QB
        modules, side, _ = inv_in.shape
        tile = (QB, examples)
        vmem = pl.BlockSpec(memory_space=pltpu.VMEM)
        hbm = pl.BlockSpec(memory_space=pltpu.HBM)
        dma = pltpu.SemaphoreType.DMA
        return pl.pallas_call(
            functools.partial(kernel, n_ex, n_x),
            out_shape=jax.ShapeDtypeStruct((3,) + tile, F32),
            in_specs=[hbm] * 5,
            out_specs=vmem,
            scratch_shapes=[
                pltpu.VMEM(inv_in.shape, BF16),
                pltpu.VMEM(inv_out.shape, BF16),
                pltpu.VMEM(listed.shape, listed.dtype),
                pltpu.VMEM((count, dims), BF16),
                pltpu.VMEM((QB, dims), BF16),
                pltpu.VMEM((3, count, dims), BF16),
                pltpu.VMEM((examples, dims), BF16),
                pltpu.VMEM((3, count, examples), F32),
                pltpu.VMEM((3, 2, n_x - 1) + tile, F32),
                pltpu.VMEM((3, 2) + tile, BF16),
                pltpu.VMEM((3, 2) + tile, BF16),
                pltpu.VMEM((modules, side, side), BF16),
                pltpu.VMEM((modules, 2 * side, 2 * side), BF16),
                pltpu.VMEM((QB * side // 2, 2 * side), F32),
                pltpu.VMEM((QB * side // 2, 2 * side), F32),
                pltpu.VMEM((listed.shape[0], listed.shape[1] * SUB), F32),
                dma((3,)),
                dma((n_chunk,)),
                dma,
                dma,
                dma,
                dma,
                dma,
                dma,
                dma((n_chunk,)),
                dma((len(PIECES),)),
                dma((3,)),
                dma((3, 2)),
                dma((2,)),
                dma((3,)),
            ],
            compiler_params=pltpu.CompilerParams(
                collective_id=0, has_side_effects=True, vmem_limit_bytes=36 * 2**20),
        )(*[pltpu.with_memory_space_constraint(v, pltpu.HBM) for v in (queries, inv_in, inv_out, store, listed)])

    in_specs = (
        P("ex", "grp"),
        P("grp", None, None),
        P("grp", None, None),
        P("ex", "grp"),
        P("ex", None),
    )
    out_specs = P(None, ("ex", "grp"), None)
    return jax.shard_map(body, mesh=mesh, in_specs=in_specs, out_specs=out_specs, check_vma=False)
```

```python
import functools

import jax
import jax.numpy as jnp
from jax import lax
from jax.experimental import pallas as pl
from jax.experimental.pallas import tpu as pltpu
from jax.sharding import PartitionSpec as P

MESH = pl.DeviceIdType.MESH
F32 = jnp.float32
BF16 = jnp.bfloat16
QB = 32
SUB = 64
SELF, PARTNER, CROSS = 0, 1, 2
GROUP = 8
PIECES = (4, 4, 4, 8, 16, 16)
SPAN = 4096


def nt_dot(a, b):
    return lax.dot_general(a, b, (((1,), (1,)), ((), ())), preferred_element_type=F32)


def iota(shape, dim):
    return lax.broadcasted_iota(jnp.int32, shape, dim)


def one_hot(cond):
    return jnp.where(cond, 1.0, 0.0).astype(BF16)


def place(a, b):
    return jnp.dot(a, b, preferred_element_type=F32).astype(BF16)


def split_factor(matrix, side):
    half = side // 2
    row = iota((side, side), 0)
    col = iota((side, side), 1)
    rows = one_hot(col == 2 * (row % half) + row // half)
    straight = one_hot(row == 2 * (col % half) + col // half)
    swapped = one_hot(row == 2 * (col % half) + 1 - col // half)
    picked = place(rows, matrix)
    upper = place(picked, straight)
    lower = place(picked, swapped)
    return jnp.where(row < half, upper.astype(F32), lower.astype(F32)).astype(BF16)


def twice(matrix, side):
    wide = 2 * side
    rows = one_hot(iota((wide, side), 0) % side == iota((wide, side), 1))
    cols = one_hot(iota((side, wide), 0) == iota((side, wide), 1) % side)
    full = place(place(rows, matrix), cols)
    same = iota((wide, wide), 0) // side == iota((wide, wide), 1) // side
    return jnp.where(same, full.astype(F32), 0.0).astype(BF16)


def kernel(
    n_ex, n_x,
    q_hbm, in_hbm, out_hbm, s_hbm, listed_hbm, o_ref,
    in_ref, out_ref, listed_ref, raw, vraw, vis, slab, part, hop, mine, last, left_w, right_w, spread, gather, mask,
    small_sem, raw_sem, slab_sem, vraw_send, vraw_recv, near_send, near_recv, far_send, far_recv, tail_recv, hop_send, hop_recv, last_send, last_recv,
):
    modules, side, _ = in_ref.shape
    pairs = side // 2
    wide = 2 * side
    n_chunk = raw.shape[0] // QB
    depth = slab.shape[1]
    b = lax.axis_index("ex")
    g = lax.axis_index("grp")
    yl = g // n_x
    x = lax.rem(g, n_x)
    par = lax.rem(b, 2)
    partner = b + 1 - 2 * par
    cross = lax.rem(b - 1 + 2 * par + n_ex, n_ex)
    other = (1 - yl) * n_x + x

    def order(t):
        d = 1 + t // 2
        rel = lax.rem(t, 2)
        to_x = lax.rem(x + d, n_x)
        to_y = lax.rem(yl + rel, 2)
        return d, rel, to_x, to_y * n_x + to_x

    peers = [(b, other), (partner, g), (partner, other), (cross, g), (cross, other)]
    peers += [(b, yl * n_x + lax.rem(x + d, n_x)) for d in range(1, n_x)]
    barrier = pltpu.get_barrier_semaphore()
    for peer in peers:
        pl.semaphore_signal(barrier, inc=1, device_id=peer, device_id_type=MESH)

    def rows_of(t):
        return pl.ds(pl.multiple_of(order(t)[3] * QB, QB), QB)

    def load_raw(t):
        return pltpu.make_async_copy(q_hbm.at[rows_of(t)], raw.at[rows_of(t)], raw_sem.at[t])

    small = [
        pltpu.make_async_copy(source, target, small_sem.at[i])
        for i, (source, target) in enumerate([(in_hbm, in_ref), (out_hbm, out_ref), (listed_hbm, listed_ref)])
    ]
    for copy in small:
        copy.start()
    for i in range(n_chunk):
        load_raw((i + 1) % n_chunk).start()
    slab_copy = pltpu.make_async_copy(s_hbm, slab, slab_sem)
    slab_copy.start()

    pl.semaphore_wait(barrier, len(peers))

    raw_out = pltpu.make_async_remote_copy(
        q_hbm.at[rows_of(0)], vraw, vraw_send, vraw_recv,
        device_id=(cross, g), device_id_type=MESH)
    raw_out.start()

    for copy in small:
        copy.wait()
    for m in range(modules):
        left_w[m] = split_factor(in_ref[m], side)
        right_w[m] = twice(out_ref[m], side)
    row = jnp.sum(
        jnp.where(iota(listed_ref.shape, 0) == g, listed_ref[...].astype(F32), 0.0), axis=0, keepdims=True)
    fan_shape = (listed_ref.shape[1], mask.shape[1])
    fan = one_hot(iota(fan_shape, 1) // SUB == iota(fan_shape, 0))
    mask[...] = jnp.dot(
        jnp.broadcast_to(row, listed_ref.shape).astype(BF16), fan, preferred_element_type=F32)

    low = (iota((pairs, GROUP * wide), 1) % wide) < side

    def precondition(src, dst):
        for m in range(modules):
            base = m * side * side
            for p in range(pairs):
                spread[pl.ds(p, QB, stride=pairs), :] = src[:, base + p * wide:base + (p + 1) * wide].astype(F32)
            for q in range(0, QB, GROUP):
                rows = spread[q * pairs:(q + GROUP) * pairs, :]
                turned = pltpu.roll(rows, side, 1).astype(BF16)
                rows = rows.astype(BF16)
                lay = lambda v: jnp.concatenate([v[i * pairs:(i + 1) * pairs] for i in range(GROUP)], axis=1)
                both = jnp.concatenate([lay(rows), lay(turned)], axis=0)
                left = jnp.dot(left_w[m], both, preferred_element_type=F32)
                left = jnp.where(low, left[:pairs], left[pairs:]).astype(BF16)
                stack = jnp.concatenate([left[:, i * wide:(i + 1) * wide] for i in range(GROUP)], axis=0)
                gather[q * pairs:(q + GROUP) * pairs, :] = jnp.dot(stack, right_w[m], preferred_element_type=F32)
            for p in range(pairs):
                dst[:, base + p * wide:base + (p + 1) * wide] = gather[pl.ds(p, QB, stride=pairs), :].astype(BF16)

    def to_partner(rows):
        return pltpu.make_async_remote_copy(
            vis.at[SELF, rows], vis.at[PARTNER, rows], near_send, near_recv,
            device_id=(partner, g), device_id_type=MESH)

    def to_cross(t):
        return pltpu.make_async_remote_copy(
            vis.at[SELF, rows_of(t)], vis.at[CROSS, rows_of(t)], far_send, far_recv.at[t],
            device_id=(cross, g), device_id_type=MESH)

    widths = [depth // fraction for fraction in PIECES]
    cuts = [slice(sum(widths[:k]), sum(widths[:k + 1])) for k in range(len(widths))]

    def tail_piece(k):
        at = rows_of(n_chunk - 1), cuts[k]
        return pltpu.make_async_remote_copy(
            vis.at[(SELF,) + at], vis.at[(CROSS,) + at], far_send, tail_recv.at[k],
            device_id=(cross, g), device_id_type=MESH)

    def prepare(i, carry):
        t = lax.rem(i + 1, n_chunk)
        load_raw(t).wait()
        precondition(raw.at[rows_of(t)], vis.at[SELF, rows_of(t)])

        @pl.when(jnp.logical_and(t > 0, t < n_chunk - 1))
        def _():
            to_cross(t).start()

        @pl.when(t == n_chunk - 1)
        def _():
            for k in range(len(cuts)):
                tail_piece(k).start()

        to_partner(rows_of(t)).start()
        return carry

    lax.fori_loop(0, n_chunk, prepare, 0)
    slab_copy.wait()

    def to_hop(w, t):
        d, rel, to_x, j = order(t)
        return pltpu.make_async_remote_copy(
            part.at[w, rows_of(t)], hop.at[w, rel, n_x - 1 - d], hop_send.at[w], hop_recv.at[w, rel],
            device_id=(b, yl * n_x + to_x), device_id_type=MESH)

    spans = [slice(at, at + SPAN) for at in range(0, depth, SPAN)]

    def score_all(w):
        for at in spans:
            product = nt_dot(vis[w, :, at], slab[:, at])
            part[w] = product if at.start == 0 else part[w] + product

        def send(t, carry):
            to_hop(w, t).start()
            return carry

        lax.fori_loop(0, n_chunk - 2, send, 0)

    def far(t):
        rows = rows_of(t)
        part[CROSS, rows] = sum(nt_dot(vis[CROSS, rows, at], slab[:, at]) for at in spans)

    def far_pieces(t):
        rows = rows_of(t)
        for k, at in enumerate(cuts):
            tail_piece(k).wait_recv()
            product = nt_dot(vis[CROSS, rows, at], slab[:, at])
            part[CROSS, rows] = product if k == 0 else part[CROSS, rows] + product

    def far_step(t, carry):
        @pl.when(t > 0)
        def _():
            to_cross(t).wait_recv()

        far(t)

        @pl.when(t < n_chunk - 2)
        def _():
            to_hop(CROSS, t).start()

        return carry

    owner = (b, partner, cross)

    def to_last(w, rel):
        return pltpu.make_async_remote_copy(
            mine.at[w, rel], last.at[w, rel], last_send.at[min(w, 1)], last_recv.at[w],
            device_id=(owner[w], g if rel == 0 else other), device_id_type=MESH)

    def group(ref, send, recv):
        return pltpu.make_async_remote_copy(
            ref, ref, send, recv, device_id=(partner, g), device_id_type=MESH)

    def gather_x(w, rel):
        group(hop.at[w, rel], hop_send.at[w], hop_recv.at[w, rel]).wait_recv()
        rows = rows_of(n_chunk - 2 + rel)
        total = part[w, rows]
        for d in range(n_x - 1):
            total = total + hop[w, rel, d]
        if w == SELF and rel == 0:
            part[w, rows] = total
        else:
            mine[w, rel] = total.astype(mine.dtype)
            to_last(w, rel).start()

    def finish(w):
        width = part.shape[2]
        if w == SELF:
            to_last(w, 1).wait_recv()
            total = part[w, rows_of(n_chunk - 2)] + last[w, 1].astype(F32)
            o_ref[1] = total * mask[0:1, width:2 * width]
            return
        group(last.at[w], last_send.at[1], last_recv.at[w]).wait_recv()
        total = last[w, 0].astype(F32) + last[w, 1].astype(F32)
        upper = par == (1 if w == CROSS else 0)

        @pl.when(upper)
        def _():
            o_ref[2] = total * mask[0:1, 2 * width:3 * width]

        @pl.when(jnp.logical_not(upper))
        def _():
            o_ref[0] = total * mask[0:1, 0:width]

    score_all(SELF)
    to_partner(slice(None)).wait_recv()
    score_all(PARTNER)

    for w in (SELF, PARTNER):
        for rel in range(2):
            gather_x(w, rel)

    raw_out.wait_recv()
    precondition(vraw, vis.at[CROSS, rows_of(0)])
    lax.fori_loop(0, n_chunk - 1, far_step, 0)
    gather_x(CROSS, 0)
    far_pieces(n_chunk - 1)
    gather_x(CROSS, 1)
    finish(SELF)
    finish(PARTNER)

    raw_out.wait_send()
    to_partner(slice(None)).wait_send()
    group(vis.at[SELF, 0:(n_chunk - 1) * QB], far_send, far_recv.at[0]).wait_send()
    for w in range(3):
        group(part.at[w, 0:(n_chunk - 2) * QB], hop_send.at[w], hop_recv.at[w, 0]).wait_send()
    to_last(SELF, 1).wait_send()
    group(mine.at[1:3], last_send.at[1], last_recv.at[1]).wait_send()
    finish(CROSS)


def solution(mesh):
    n_ex = mesh.shape["ex"]
    n_grp = mesh.shape["grp"]
    n_x = n_grp // 2

    def body(queries, inv_in, inv_out, store, listed):
        count, dims = queries.shape
        examples = store.shape[0]
        n_chunk = count // QB
        modules, side, _ = inv_in.shape
        tile = (QB, examples)
        vmem = pl.BlockSpec(memory_space=pltpu.VMEM)
        hbm = pl.BlockSpec(memory_space=pltpu.HBM)
        dma = pltpu.SemaphoreType.DMA
        return pl.pallas_call(
            functools.partial(kernel, n_ex, n_x),
            out_shape=jax.ShapeDtypeStruct((3,) + tile, F32),
            in_specs=[hbm] * 5,
            out_specs=vmem,
            scratch_shapes=[
                pltpu.VMEM(inv_in.shape, BF16),
                pltpu.VMEM(inv_out.shape, BF16),
                pltpu.VMEM(listed.shape, listed.dtype),
                pltpu.VMEM((count, dims), BF16),
                pltpu.VMEM((QB, dims), BF16),
                pltpu.VMEM((3, count, dims), BF16),
                pltpu.VMEM((examples, dims), BF16),
                pltpu.VMEM((3, count, examples), F32),
                pltpu.VMEM((3, 2, n_x - 1) + tile, F32),
                pltpu.VMEM((3, 2) + tile, BF16),
                pltpu.VMEM((3, 2) + tile, BF16),
                pltpu.VMEM((modules, side, side), BF16),
                pltpu.VMEM((modules, 2 * side, 2 * side), BF16),
                pltpu.VMEM((QB * side // 2, 2 * side), F32),
                pltpu.VMEM((QB * side // 2, 2 * side), F32),
                pltpu.VMEM((listed.shape[0], listed.shape[1] * SUB), F32),
                dma((3,)),
                dma((n_chunk,)),
                dma,
                dma,
                dma,
                dma,
                dma,
                dma,
                dma((n_chunk,)),
                dma((len(PIECES),)),
                dma((3,)),
                dma((3, 2)),
                dma((2,)),
                dma((3,)),
            ],
            compiler_params=pltpu.CompilerParams(
                collective_id=0, has_side_effects=True, vmem_limit_bytes=36 * 2**20),
        )(*[pltpu.with_memory_space_constraint(v, pltpu.HBM) for v in (queries, inv_in, inv_out, store, listed)])

    in_specs = (
        P("ex", "grp"),
        P("grp", None, None),
        P("grp", None, None),
        P("ex", "grp"),
        P("ex", None),
    )
    out_specs = P(None, ("ex", "grp"), None)
    return jax.shard_map(body, mesh=mesh, in_specs=in_specs, out_specs=out_specs, check_vma=False)
```

```python
import functools

import jax
import jax.numpy as jnp
from jax import lax
from jax.experimental import pallas as pl
from jax.experimental.pallas import tpu as pltpu
from jax.sharding import PartitionSpec as P

MESH = pl.DeviceIdType.MESH
F32 = jnp.float32
BF16 = jnp.bfloat16
QB = 32
SUB = 64
SELF, PARTNER, CROSS = 0, 1, 2
GROUP = 8
PIECES = (4, 4, 4, 8, 16, 16)
SPAN = 4096


def nt_dot(a, b):
    return lax.dot_general(a, b, (((1,), (1,)), ((), ())), preferred_element_type=F32)


def iota(shape, dim):
    return lax.broadcasted_iota(jnp.int32, shape, dim)


def one_hot(cond):
    return jnp.where(cond, 1.0, 0.0).astype(BF16)


def place(a, b):
    return jnp.dot(a, b, preferred_element_type=F32).astype(BF16)


def split_factor(matrix, side):
    half = side // 2
    row = iota((side, side), 0)
    col = iota((side, side), 1)
    rows = one_hot(col == 2 * (row % half) + row // half)
    straight = one_hot(row == 2 * (col % half) + col // half)
    swapped = one_hot(row == 2 * (col % half) + 1 - col // half)
    picked = place(rows, matrix)
    upper = place(picked, straight)
    lower = place(picked, swapped)
    return jnp.where(row < half, upper.astype(F32), lower.astype(F32)).astype(BF16)


def twice(matrix, side):
    wide = 2 * side
    rows = one_hot(iota((wide, side), 0) % side == iota((wide, side), 1))
    cols = one_hot(iota((side, wide), 0) == iota((side, wide), 1) % side)
    full = place(place(rows, matrix), cols)
    same = iota((wide, wide), 0) // side == iota((wide, wide), 1) // side
    return jnp.where(same, full.astype(F32), 0.0).astype(BF16)


def kernel(
    n_ex, n_x,
    q_hbm, in_hbm, out_hbm, s_hbm, listed_hbm, o_ref,
    in_ref, out_ref, listed_ref, raw, vraw, vis, slab, part, hop, mine, last, left_w, right_w, spread, gather, mask,
    small_sem, raw_sem, slab_sem, vraw_send, vraw_recv, near_send, near_recv, far_send, far_recv, tail_recv, hop_send, hop_recv, last_send, last_recv,
):
    modules, side, _ = in_ref.shape
    pairs = side // 2
    wide = 2 * side
    n_chunk = raw.shape[0] // QB
    depth = slab.shape[1]
    b = lax.axis_index("ex")
    g = lax.axis_index("grp")
    yl = g // n_x
    x = lax.rem(g, n_x)
    par = lax.rem(b, 2)
    partner = b + 1 - 2 * par
    cross = lax.rem(b - 1 + 2 * par + n_ex, n_ex)
    other = (1 - yl) * n_x + x

    def order(t):
        d = 1 + t // 2
        rel = lax.rem(t, 2)
        to_x = lax.rem(x + d, n_x)
        to_y = lax.rem(yl + rel, 2)
        return d, rel, to_x, to_y * n_x + to_x

    peers = [(b, other), (partner, g), (partner, other), (cross, g), (cross, other)]
    peers += [(b, yl * n_x + lax.rem(x + d, n_x)) for d in range(1, n_x)]
    barrier = pltpu.get_barrier_semaphore()
    for peer in peers:
        pl.semaphore_signal(barrier, inc=1, device_id=peer, device_id_type=MESH)

    def rows_of(t):
        return pl.ds(pl.multiple_of(order(t)[3] * QB, QB), QB)

    def load_raw(t):
        return pltpu.make_async_copy(q_hbm.at[rows_of(t)], raw.at[rows_of(t)], raw_sem.at[t])

    small = [
        pltpu.make_async_copy(source, target, small_sem.at[i])
        for i, (source, target) in enumerate([(in_hbm, in_ref), (out_hbm, out_ref), (listed_hbm, listed_ref)])
    ]
    for copy in small:
        copy.start()
    for i in range(n_chunk):
        load_raw((i + 1) % n_chunk).start()
    slab_copy = pltpu.make_async_copy(s_hbm, slab, slab_sem)
    slab_copy.start()

    pl.semaphore_wait(barrier, len(peers))

    raw_out = pltpu.make_async_remote_copy(
        q_hbm.at[rows_of(0)], vraw, vraw_send, vraw_recv,
        device_id=(cross, g), device_id_type=MESH)
    raw_out.start()

    for copy in small:
        copy.wait()
    for m in range(modules):
        left_w[m] = split_factor(in_ref[m], side)
        right_w[m] = twice(out_ref[m], side)
    row = jnp.sum(
        jnp.where(iota(listed_ref.shape, 0) == g, listed_ref[...].astype(F32), 0.0), axis=0, keepdims=True)
    fan_shape = (listed_ref.shape[1], mask.shape[1])
    fan = one_hot(iota(fan_shape, 1) // SUB == iota(fan_shape, 0))
    mask[...] = jnp.dot(
        jnp.broadcast_to(row, listed_ref.shape).astype(BF16), fan, preferred_element_type=F32)

    low = (iota((pairs, GROUP * wide), 1) % wide) < side

    def precondition(src, dst):
        for m in range(modules):
            base = m * side * side
            for p in range(pairs):
                spread[pl.ds(p, QB, stride=pairs), :] = src[:, base + p * wide:base + (p + 1) * wide].astype(F32)
            for q in range(0, QB, GROUP):
                rows = spread[q * pairs:(q + GROUP) * pairs, :]
                turned = pltpu.roll(rows, side, 1).astype(BF16)
                rows = rows.astype(BF16)
                lay = lambda v: jnp.concatenate([v[i * pairs:(i + 1) * pairs] for i in range(GROUP)], axis=1)
                both = jnp.concatenate([lay(rows), lay(turned)], axis=0)
                left = jnp.dot(left_w[m], both, preferred_element_type=F32)
                left = jnp.where(low, left[:pairs], left[pairs:]).astype(BF16)
                stack = jnp.concatenate([left[:, i * wide:(i + 1) * wide] for i in range(GROUP)], axis=0)
                gather[q * pairs:(q + GROUP) * pairs, :] = jnp.dot(stack, right_w[m], preferred_element_type=F32)
            for p in range(pairs):
                dst[:, base + p * wide:base + (p + 1) * wide] = gather[pl.ds(p, QB, stride=pairs), :].astype(BF16)

    def to_partner(rows):
        return pltpu.make_async_remote_copy(
            vis.at[SELF, rows], vis.at[PARTNER, rows], near_send, near_recv,
            device_id=(partner, g), device_id_type=MESH)

    def to_cross(t):
        return pltpu.make_async_remote_copy(
            vis.at[SELF, rows_of(t)], vis.at[CROSS, rows_of(t)], far_send, far_recv.at[t],
            device_id=(cross, g), device_id_type=MESH)

    widths = [depth // fraction for fraction in PIECES]
    cuts = [slice(sum(widths[:k]), sum(widths[:k + 1])) for k in range(len(widths))]

    def tail_piece(k):
        at = rows_of(n_chunk - 1), cuts[k]
        return pltpu.make_async_remote_copy(
            vis.at[(SELF,) + at], vis.at[(CROSS,) + at], far_send, tail_recv.at[k],
            device_id=(cross, g), device_id_type=MESH)

    def prepare(i, carry):
        t = lax.rem(i + 1, n_chunk)
        load_raw(t).wait()
        precondition(raw.at[rows_of(t)], vis.at[SELF, rows_of(t)])

        @pl.when(jnp.logical_and(t > 0, t < n_chunk - 1))
        def _():
            to_cross(t).start()

        @pl.when(t == n_chunk - 1)
        def _():
            for k in range(len(cuts)):
                tail_piece(k).start()

        to_partner(rows_of(t)).start()
        return carry

    lax.fori_loop(0, n_chunk, prepare, 0)
    slab_copy.wait()

    def to_hop(w, t):
        d, rel, to_x, j = order(t)
        return pltpu.make_async_remote_copy(
            part.at[w, rows_of(t)], hop.at[w, rel, n_x - 1 - d], hop_send.at[w], hop_recv.at[w, rel],
            device_id=(b, yl * n_x + to_x), device_id_type=MESH)

    spans = [slice(at, at + SPAN) for at in range(0, depth, SPAN)]

    def score_all(w):
        for at in spans:
            product = nt_dot(vis[w, :, at], slab[:, at])
            part[w] = product if at.start == 0 else part[w] + product

        def send(t, carry):
            to_hop(w, t).start()
            return carry

        lax.fori_loop(0, n_chunk - 2, send, 0)

    def far(t):
        rows = rows_of(t)
        part[CROSS, rows] = sum(nt_dot(vis[CROSS, rows, at], slab[:, at]) for at in spans)

    def far_pieces(t):
        rows = rows_of(t)
        for k, at in enumerate(cuts):
            tail_piece(k).wait_recv()
            product = nt_dot(vis[CROSS, rows, at], slab[:, at])
            part[CROSS, rows] = product if k == 0 else part[CROSS, rows] + product

    def far_step(t, carry):
        @pl.when(t > 0)
        def _():
            to_cross(t).wait_recv()

        far(t)

        @pl.when(t < n_chunk - 2)
        def _():
            to_hop(CROSS, t).start()

        return carry

    owner = (b, partner, cross)

    def to_last(w, rel):
        return pltpu.make_async_remote_copy(
            mine.at[w, rel], last.at[w, rel], last_send.at[min(w, 1)], last_recv.at[w],
            device_id=(owner[w], g if rel == 0 else other), device_id_type=MESH)

    def group(ref, send, recv):
        return pltpu.make_async_remote_copy(
            ref, ref, send, recv, device_id=(partner, g), device_id_type=MESH)

    def gather_x(w, rel):
        group(hop.at[w, rel], hop_send.at[w], hop_recv.at[w, rel]).wait_recv()
        rows = rows_of(n_chunk - 2 + rel)
        total = part[w, rows]
        for d in range(n_x - 1):
            total = total + hop[w, rel, d]
        if w == SELF and rel == 0:
            part[w, rows] = total
        else:
            mine[w, rel] = total.astype(mine.dtype)
            to_last(w, rel).start()

    def finish(w):
        width = part.shape[2]
        if w == SELF:
            to_last(w, 1).wait_recv()
            total = part[w, rows_of(n_chunk - 2)] + last[w, 1].astype(F32)
            o_ref[1] = total * mask[0:1, width:2 * width]
            return
        group(last.at[w], last_send.at[1], last_recv.at[w]).wait_recv()
        total = last[w, 0].astype(F32) + last[w, 1].astype(F32)
        upper = par == (1 if w == CROSS else 0)

        @pl.when(upper)
        def _():
            o_ref[2] = total * mask[0:1, 2 * width:3 * width]

        @pl.when(jnp.logical_not(upper))
        def _():
            o_ref[0] = total * mask[0:1, 0:width]

    score_all(SELF)
    to_partner(slice(None)).wait_recv()
    score_all(PARTNER)

    raw_out.wait_recv()
    precondition(vraw, vis.at[CROSS, rows_of(0)])
    lax.fori_loop(0, n_chunk - 1, far_step, 0)
    gather_x(CROSS, 0)
    far_pieces(n_chunk - 1)
    gather_x(CROSS, 1)
    for w in (SELF, PARTNER):
        for rel in range(2):
            gather_x(w, rel)
    finish(SELF)
    finish(PARTNER)

    raw_out.wait_send()
    to_partner(slice(None)).wait_send()
    group(vis.at[SELF, 0:(n_chunk - 1) * QB], far_send, far_recv.at[0]).wait_send()
    for w in range(3):
        group(part.at[w, 0:(n_chunk - 2) * QB], hop_send.at[w], hop_recv.at[w, 0]).wait_send()
    to_last(SELF, 1).wait_send()
    group(mine.at[1:3], last_send.at[1], last_recv.at[1]).wait_send()
    finish(CROSS)


def solution(mesh):
    n_ex = mesh.shape["ex"]
    n_grp = mesh.shape["grp"]
    n_x = n_grp // 2

    def body(queries, inv_in, inv_out, store, listed):
        count, dims = queries.shape
        examples = store.shape[0]
        n_chunk = count // QB
        modules, side, _ = inv_in.shape
        tile = (QB, examples)
        vmem = pl.BlockSpec(memory_space=pltpu.VMEM)
        hbm = pl.BlockSpec(memory_space=pltpu.HBM)
        dma = pltpu.SemaphoreType.DMA
        return pl.pallas_call(
            functools.partial(kernel, n_ex, n_x),
            out_shape=jax.ShapeDtypeStruct((3,) + tile, F32),
            in_specs=[hbm] * 5,
            out_specs=vmem,
            scratch_shapes=[
                pltpu.VMEM(inv_in.shape, BF16),
                pltpu.VMEM(inv_out.shape, BF16),
                pltpu.VMEM(listed.shape, listed.dtype),
                pltpu.VMEM((count, dims), BF16),
                pltpu.VMEM((QB, dims), BF16),
                pltpu.VMEM((3, count, dims), BF16),
                pltpu.VMEM((examples, dims), BF16),
                pltpu.VMEM((3, count, examples), F32),
                pltpu.VMEM((3, 2, n_x - 1) + tile, F32),
                pltpu.VMEM((3, 2) + tile, BF16),
                pltpu.VMEM((3, 2) + tile, BF16),
                pltpu.VMEM((modules, side, side), BF16),
                pltpu.VMEM((modules, 2 * side, 2 * side), BF16),
                pltpu.VMEM((QB * side // 2, 2 * side), F32),
                pltpu.VMEM((QB * side // 2, 2 * side), F32),
                pltpu.VMEM((listed.shape[0], listed.shape[1] * SUB), F32),
                dma((3,)),
                dma((n_chunk,)),
                dma,
                dma,
                dma,
                dma,
                dma,
                dma,
                dma((n_chunk,)),
                dma((len(PIECES),)),
                dma((3,)),
                dma((3, 2)),
                dma((2,)),
                dma((3,)),
            ],
            compiler_params=pltpu.CompilerParams(
                collective_id=0, has_side_effects=True, vmem_limit_bytes=36 * 2**20),
        )(*[pltpu.with_memory_space_constraint(v, pltpu.HBM) for v in (queries, inv_in, inv_out, store, listed)])

    in_specs = (
        P("ex", "grp"),
        P("grp", None, None),
        P("grp", None, None),
        P("ex", "grp"),
        P("ex", None),
    )
    out_specs = P(None, ("ex", "grp"), None)
    return jax.shard_map(body, mesh=mesh, in_specs=in_specs, out_specs=out_specs, check_vma=False)
```

```python
import functools

import jax
import jax.numpy as jnp
from jax import lax
from jax.experimental import pallas as pl
from jax.experimental.pallas import tpu as pltpu
from jax.sharding import PartitionSpec as P

MESH = pl.DeviceIdType.MESH
F32 = jnp.float32
BF16 = jnp.bfloat16
QB = 32
SUB = 64
SELF, PARTNER, CROSS = 0, 1, 2
GROUP = 8
PIECES = (4, 4, 4, 8, 16, 16)
SPAN = 4096


def nt_dot(a, b):
    return lax.dot_general(a, b, (((1,), (1,)), ((), ())), preferred_element_type=F32)


def iota(shape, dim):
    return lax.broadcasted_iota(jnp.int32, shape, dim)


def one_hot(cond):
    return jnp.where(cond, 1.0, 0.0).astype(BF16)


def place(a, b):
    return jnp.dot(a, b, preferred_element_type=F32).astype(BF16)


def split_factor(matrix, side):
    half = side // 2
    row = iota((side, side), 0)
    col = iota((side, side), 1)
    rows = one_hot(col == 2 * (row % half) + row // half)
    straight = one_hot(row == 2 * (col % half) + col // half)
    swapped = one_hot(row == 2 * (col % half) + 1 - col // half)
    picked = place(rows, matrix)
    upper = place(picked, straight)
    lower = place(picked, swapped)
    return jnp.where(row < half, upper.astype(F32), lower.astype(F32)).astype(BF16)


def twice(matrix, side):
    wide = 2 * side
    rows = one_hot(iota((wide, side), 0) % side == iota((wide, side), 1))
    cols = one_hot(iota((side, wide), 0) == iota((side, wide), 1) % side)
    full = place(place(rows, matrix), cols)
    same = iota((wide, wide), 0) // side == iota((wide, wide), 1) // side
    return jnp.where(same, full.astype(F32), 0.0).astype(BF16)


def kernel(
    n_ex, n_x,
    q_hbm, in_hbm, out_hbm, s_hbm, listed_hbm, o_ref,
    in_ref, out_ref, listed_ref, raw, vraw, vis, slab, part, hop, mine, last, left_w, right_w, spread, gather, mask,
    small_sem, raw_sem, slab_sem, vraw_send, vraw_recv, near_send, near_recv, far_send, far_recv, tail_recv, hop_send, hop_recv, last_send, last_recv,
):
    modules, side, _ = in_ref.shape
    pairs = side // 2
    wide = 2 * side
    n_chunk = raw.shape[0] // QB
    depth = slab.shape[1]
    b = lax.axis_index("ex")
    g = lax.axis_index("grp")
    yl = g // n_x
    x = lax.rem(g, n_x)
    par = lax.rem(b, 2)
    partner = b + 1 - 2 * par
    cross = lax.rem(b - 1 + 2 * par + n_ex, n_ex)
    other = (1 - yl) * n_x + x

    def order(t):
        d = 1 + t // 2
        rel = lax.rem(t, 2)
        to_x = lax.rem(x + d, n_x)
        to_y = lax.rem(yl + rel, 2)
        return d, rel, to_x, to_y * n_x + to_x

    peers = [(b, other), (partner, g), (partner, other), (cross, g), (cross, other)]
    peers += [(b, yl * n_x + lax.rem(x + d, n_x)) for d in range(1, n_x)]
    barrier = pltpu.get_barrier_semaphore()
    for peer in peers:
        pl.semaphore_signal(barrier, inc=1, device_id=peer, device_id_type=MESH)

    def rows_of(t):
        return pl.ds(pl.multiple_of(order(t)[3] * QB, QB), QB)

    def load_raw(t):
        return pltpu.make_async_copy(q_hbm.at[rows_of(t)], raw.at[rows_of(t)], raw_sem.at[t])

    small = [
        pltpu.make_async_copy(source, target, small_sem.at[i])
        for i, (source, target) in enumerate([(in_hbm, in_ref), (out_hbm, out_ref), (listed_hbm, listed_ref)])
    ]
    for copy in small:
        copy.start()
    for i in range(n_chunk):
        load_raw((i + 1) % n_chunk).start()
    slab_copy = pltpu.make_async_copy(s_hbm, slab, slab_sem)

    pl.semaphore_wait(barrier, len(peers))

    raw_out = pltpu.make_async_remote_copy(
        q_hbm.at[rows_of(0)], vraw, vraw_send, vraw_recv,
        device_id=(cross, g), device_id_type=MESH)
    raw_out.start()
    slab_copy.start()

    for copy in small:
        copy.wait()
    for m in range(modules):
        left_w[m] = split_factor(in_ref[m], side)
        right_w[m] = twice(out_ref[m], side)
    row = jnp.sum(
        jnp.where(iota(listed_ref.shape, 0) == g, listed_ref[...].astype(F32), 0.0), axis=0, keepdims=True)
    fan_shape = (listed_ref.shape[1], mask.shape[1])
    fan = one_hot(iota(fan_shape, 1) // SUB == iota(fan_shape, 0))
    mask[...] = jnp.dot(
        jnp.broadcast_to(row, listed_ref.shape).astype(BF16), fan, preferred_element_type=F32)

    low = (iota((pairs, GROUP * wide), 1) % wide) < side

    def precondition(src, dst):
        for m in range(modules):
            base = m * side * side
            for p in range(pairs):
                spread[pl.ds(p, QB, stride=pairs), :] = src[:, base + p * wide:base + (p + 1) * wide].astype(F32)
            for q in range(0, QB, GROUP):
                rows = spread[q * pairs:(q + GROUP) * pairs, :]
                turned = pltpu.roll(rows, side, 1).astype(BF16)
                rows = rows.astype(BF16)
                lay = lambda v: jnp.concatenate([v[i * pairs:(i + 1) * pairs] for i in range(GROUP)], axis=1)
                both = jnp.concatenate([lay(rows), lay(turned)], axis=0)
                left = jnp.dot(left_w[m], both, preferred_element_type=F32)
                left = jnp.where(low, left[:pairs], left[pairs:]).astype(BF16)
                stack = jnp.concatenate([left[:, i * wide:(i + 1) * wide] for i in range(GROUP)], axis=0)
                gather[q * pairs:(q + GROUP) * pairs, :] = jnp.dot(stack, right_w[m], preferred_element_type=F32)
            for p in range(pairs):
                dst[:, base + p * wide:base + (p + 1) * wide] = gather[pl.ds(p, QB, stride=pairs), :].astype(BF16)

    def to_partner(rows):
        return pltpu.make_async_remote_copy(
            vis.at[SELF, rows], vis.at[PARTNER, rows], near_send, near_recv,
            device_id=(partner, g), device_id_type=MESH)

    def to_cross(t):
        return pltpu.make_async_remote_copy(
            vis.at[SELF, rows_of(t)], vis.at[CROSS, rows_of(t)], far_send, far_recv.at[t],
            device_id=(cross, g), device_id_type=MESH)

    widths = [depth // fraction for fraction in PIECES]
    cuts = [slice(sum(widths[:k]), sum(widths[:k + 1])) for k in range(len(widths))]

    def tail_piece(k):
        at = rows_of(n_chunk - 1), cuts[k]
        return pltpu.make_async_remote_copy(
            vis.at[(SELF,) + at], vis.at[(CROSS,) + at], far_send, tail_recv.at[k],
            device_id=(cross, g), device_id_type=MESH)

    def prepare(i, carry):
        t = lax.rem(i + 1, n_chunk)
        load_raw(t).wait()
        precondition(raw.at[rows_of(t)], vis.at[SELF, rows_of(t)])

        @pl.when(jnp.logical_and(t > 0, t < n_chunk - 1))
        def _():
            to_cross(t).start()

        @pl.when(t == n_chunk - 1)
        def _():
            for k in range(len(cuts)):
                tail_piece(k).start()

        to_partner(rows_of(t)).start()
        return carry

    lax.fori_loop(0, n_chunk, prepare, 0)
    slab_copy.wait()

    def to_hop(w, t):
        d, rel, to_x, j = order(t)
        return pltpu.make_async_remote_copy(
            part.at[w, rows_of(t)], hop.at[w, rel, n_x - 1 - d], hop_send.at[w], hop_recv.at[w, rel],
            device_id=(b, yl * n_x + to_x), device_id_type=MESH)

    spans = [slice(at, at + SPAN) for at in range(0, depth, SPAN)]

    def score_all(w):
        for at in spans:
            product = nt_dot(vis[w, :, at], slab[:, at])
            part[w] = product if at.start == 0 else part[w] + product

        def send(t, carry):
            to_hop(w, t).start()
            return carry

        lax.fori_loop(0, n_chunk - 2, send, 0)

    def far(t):
        rows = rows_of(t)
        part[CROSS, rows] = sum(nt_dot(vis[CROSS, rows, at], slab[:, at]) for at in spans)

    def far_pieces(t):
        rows = rows_of(t)
        for k, at in enumerate(cuts):
            tail_piece(k).wait_recv()
            product = nt_dot(vis[CROSS, rows, at], slab[:, at])
            part[CROSS, rows] = product if k == 0 else part[CROSS, rows] + product

    def far_step(t, carry):
        @pl.when(t > 0)
        def _():
            to_cross(t).wait_recv()

        far(t)

        @pl.when(t < n_chunk - 2)
        def _():
            to_hop(CROSS, t).start()

        return carry

    owner = (b, partner, cross)

    def to_last(w, rel):
        return pltpu.make_async_remote_copy(
            mine.at[w, rel], last.at[w, rel], last_send.at[min(w, 1)], last_recv.at[w],
            device_id=(owner[w], g if rel == 0 else other), device_id_type=MESH)

    def group(ref, send, recv):
        return pltpu.make_async_remote_copy(
            ref, ref, send, recv, device_id=(partner, g), device_id_type=MESH)

    def gather_x(w, rel):
        group(hop.at[w, rel], hop_send.at[w], hop_recv.at[w, rel]).wait_recv()
        rows = rows_of(n_chunk - 2 + rel)
        total = part[w, rows]
        for d in range(n_x - 1):
            total = total + hop[w, rel, d]
        if w == SELF and rel == 0:
            part[w, rows] = total
        else:
            mine[w, rel] = total.astype(mine.dtype)
            to_last(w, rel).start()

    def finish(w):
        width = part.shape[2]
        if w == SELF:
            to_last(w, 1).wait_recv()
            total = part[w, rows_of(n_chunk - 2)] + last[w, 1].astype(F32)
            o_ref[1] = total * mask[0:1, width:2 * width]
            return
        group(last.at[w], last_send.at[1], last_recv.at[w]).wait_recv()
        total = last[w, 0].astype(F32) + last[w, 1].astype(F32)
        upper = par == (1 if w == CROSS else 0)

        @pl.when(upper)
        def _():
            o_ref[2] = total * mask[0:1, 2 * width:3 * width]

        @pl.when(jnp.logical_not(upper))
        def _():
            o_ref[0] = total * mask[0:1, 0:width]

    score_all(SELF)
    to_partner(slice(None)).wait_recv()
    score_all(PARTNER)

    raw_out.wait_recv()
    precondition(vraw, vis.at[CROSS, rows_of(0)])
    lax.fori_loop(0, n_chunk - 1, far_step, 0)
    gather_x(CROSS, 0)
    far_pieces(n_chunk - 1)
    gather_x(CROSS, 1)
    for w in (SELF, PARTNER):
        for rel in range(2):
            gather_x(w, rel)
    finish(SELF)
    finish(PARTNER)

    raw_out.wait_send()
    to_partner(slice(None)).wait_send()
    group(vis.at[SELF, 0:(n_chunk - 1) * QB], far_send, far_recv.at[0]).wait_send()
    for w in range(3):
        group(part.at[w, 0:(n_chunk - 2) * QB], hop_send.at[w], hop_recv.at[w, 0]).wait_send()
    to_last(SELF, 1).wait_send()
    group(mine.at[1:3], last_send.at[1], last_recv.at[1]).wait_send()
    finish(CROSS)


def solution(mesh):
    n_ex = mesh.shape["ex"]
    n_grp = mesh.shape["grp"]
    n_x = n_grp // 2

    def body(queries, inv_in, inv_out, store, listed):
        count, dims = queries.shape
        examples = store.shape[0]
        n_chunk = count // QB
        modules, side, _ = inv_in.shape
        tile = (QB, examples)
        vmem = pl.BlockSpec(memory_space=pltpu.VMEM)
        hbm = pl.BlockSpec(memory_space=pltpu.HBM)
        dma = pltpu.SemaphoreType.DMA
        return pl.pallas_call(
            functools.partial(kernel, n_ex, n_x),
            out_shape=jax.ShapeDtypeStruct((3,) + tile, F32),
            in_specs=[hbm] * 5,
            out_specs=vmem,
            scratch_shapes=[
                pltpu.VMEM(inv_in.shape, BF16),
                pltpu.VMEM(inv_out.shape, BF16),
                pltpu.VMEM(listed.shape, listed.dtype),
                pltpu.VMEM((count, dims), BF16),
                pltpu.VMEM((QB, dims), BF16),
                pltpu.VMEM((3, count, dims), BF16),
                pltpu.VMEM((examples, dims), BF16),
                pltpu.VMEM((3, count, examples), F32),
                pltpu.VMEM((3, 2, n_x - 1) + tile, F32),
                pltpu.VMEM((3, 2) + tile, BF16),
                pltpu.VMEM((3, 2) + tile, BF16),
                pltpu.VMEM((modules, side, side), BF16),
                pltpu.VMEM((modules, 2 * side, 2 * side), BF16),
                pltpu.VMEM((QB * side // 2, 2 * side), F32),
                pltpu.VMEM((QB * side // 2, 2 * side), F32),
                pltpu.VMEM((listed.shape[0], listed.shape[1] * SUB), F32),
                dma((3,)),
                dma((n_chunk,)),
                dma,
                dma,
                dma,
                dma,
                dma,
                dma,
                dma((n_chunk,)),
                dma((len(PIECES),)),
                dma((3,)),
                dma((3, 2)),
                dma((2,)),
                dma((3,)),
            ],
            compiler_params=pltpu.CompilerParams(
                collective_id=0, has_side_effects=True, vmem_limit_bytes=36 * 2**20),
        )(*[pltpu.with_memory_space_constraint(v, pltpu.HBM) for v in (queries, inv_in, inv_out, store, listed)])

    in_specs = (
        P("ex", "grp"),
        P("grp", None, None),
        P("grp", None, None),
        P("ex", "grp"),
        P("ex", None),
    )
    out_specs = P(None, ("ex", "grp"), None)
    return jax.shard_map(body, mesh=mesh, in_specs=in_specs, out_specs=out_specs, check_vma=False)
```

```python
import functools

import jax
import jax.numpy as jnp
from jax import lax
from jax.experimental import pallas as pl
from jax.experimental.pallas import tpu as pltpu
from jax.sharding import PartitionSpec as P

MESH = pl.DeviceIdType.MESH
F32 = jnp.float32
BF16 = jnp.bfloat16
QB = 32
SUB = 64
SELF, PARTNER, CROSS = 0, 1, 2
GROUP = 8
PIECES = (4, 4, 4, 8, 16, 16)
SPAN = 4096


def nt_dot(a, b):
    return lax.dot_general(a, b, (((1,), (1,)), ((), ())), preferred_element_type=F32)


def iota(shape, dim):
    return lax.broadcasted_iota(jnp.int32, shape, dim)


def one_hot(cond):
    return jnp.where(cond, 1.0, 0.0).astype(BF16)


def place(a, b):
    return jnp.dot(a, b, preferred_element_type=F32).astype(BF16)


def split_factor(matrix, side):
    half = side // 2
    row = iota((side, side), 0)
    col = iota((side, side), 1)
    rows = one_hot(col == 2 * (row % half) + row // half)
    straight = one_hot(row == 2 * (col % half) + col // half)
    swapped = one_hot(row == 2 * (col % half) + 1 - col // half)
    picked = place(rows, matrix)
    upper = place(picked, straight)
    lower = place(picked, swapped)
    return jnp.where(row < half, upper.astype(F32), lower.astype(F32)).astype(BF16)


def twice(matrix, side):
    wide = 2 * side
    rows = one_hot(iota((wide, side), 0) % side == iota((wide, side), 1))
    cols = one_hot(iota((side, wide), 0) == iota((side, wide), 1) % side)
    full = place(place(rows, matrix), cols)
    same = iota((wide, wide), 0) // side == iota((wide, wide), 1) // side
    return jnp.where(same, full.astype(F32), 0.0).astype(BF16)


def kernel(
    n_ex, n_x,
    q_hbm, in_hbm, out_hbm, s_hbm, listed_hbm, o_ref,
    in_ref, out_ref, listed_ref, raw, vraw, vis, slab, part, hop, mine, last, left_w, right_w, spread, gather, mask,
    small_sem, raw_sem, slab_sem, vraw_send, vraw_recv, near_send, near_recv, far_send, far_recv, tail_recv, hop_send, hop_recv, last_send, last_recv,
):
    modules, side, _ = in_ref.shape
    pairs = side // 2
    wide = 2 * side
    n_chunk = raw.shape[0] // QB
    depth = slab.shape[1]
    b = lax.axis_index("ex")
    g = lax.axis_index("grp")
    yl = g // n_x
    x = lax.rem(g, n_x)
    par = lax.rem(b, 2)
    partner = b + 1 - 2 * par
    cross = lax.rem(b - 1 + 2 * par + n_ex, n_ex)
    other = (1 - yl) * n_x + x

    def order(t):
        d = 1 + t // 2
        rel = lax.rem(t, 2)
        to_x = lax.rem(x + d, n_x)
        to_y = lax.rem(yl + rel, 2)
        return d, rel, to_x, to_y * n_x + to_x

    peers = [(b, other), (partner, g), (partner, other), (cross, g), (cross, other)]
    peers += [(b, yl * n_x + lax.rem(x + d, n_x)) for d in range(1, n_x)]
    barrier = pltpu.get_barrier_semaphore()
    for peer in peers:
        pl.semaphore_signal(barrier, inc=1, device_id=peer, device_id_type=MESH)

    def rows_of(t):
        return pl.ds(pl.multiple_of(order(t)[3] * QB, QB), QB)

    def load_raw(t):
        return pltpu.make_async_copy(q_hbm.at[rows_of(t)], raw.at[rows_of(t)], raw_sem.at[t])

    small = [
        pltpu.make_async_copy(source, target, small_sem.at[i])
        for i, (source, target) in enumerate([(in_hbm, in_ref), (out_hbm, out_ref), (listed_hbm, listed_ref)])
    ]
    for copy in small:
        copy.start()
    for i in range(2):
        load_raw((i + 1) % n_chunk).start()
    slab_copy = pltpu.make_async_copy(s_hbm, slab, slab_sem)

    pl.semaphore_wait(barrier, len(peers))

    raw_out = pltpu.make_async_remote_copy(
        q_hbm.at[rows_of(0)], vraw, vraw_send, vraw_recv,
        device_id=(cross, g), device_id_type=MESH)
    raw_out.start()
    for i in range(2, n_chunk):
        load_raw((i + 1) % n_chunk).start()
    slab_copy.start()

    for copy in small:
        copy.wait()
    for m in range(modules):
        left_w[m] = split_factor(in_ref[m], side)
        right_w[m] = twice(out_ref[m], side)
    row = jnp.sum(
        jnp.where(iota(listed_ref.shape, 0) == g, listed_ref[...].astype(F32), 0.0), axis=0, keepdims=True)
    fan_shape = (listed_ref.shape[1], mask.shape[1])
    fan = one_hot(iota(fan_shape, 1) // SUB == iota(fan_shape, 0))
    mask[...] = jnp.dot(
        jnp.broadcast_to(row, listed_ref.shape).astype(BF16), fan, preferred_element_type=F32)

    low = (iota((pairs, GROUP * wide), 1) % wide) < side

    def precondition(src, dst):
        for m in range(modules):
            base = m * side * side
            for p in range(pairs):
                spread[pl.ds(p, QB, stride=pairs), :] = src[:, base + p * wide:base + (p + 1) * wide].astype(F32)
            for q in range(0, QB, GROUP):
                rows = spread[q * pairs:(q + GROUP) * pairs, :]
                turned = pltpu.roll(rows, side, 1).astype(BF16)
                rows = rows.astype(BF16)
                lay = lambda v: jnp.concatenate([v[i * pairs:(i + 1) * pairs] for i in range(GROUP)], axis=1)
                both = jnp.concatenate([lay(rows), lay(turned)], axis=0)
                left = jnp.dot(left_w[m], both, preferred_element_type=F32)
                left = jnp.where(low, left[:pairs], left[pairs:]).astype(BF16)
                stack = jnp.concatenate([left[:, i * wide:(i + 1) * wide] for i in range(GROUP)], axis=0)
                gather[q * pairs:(q + GROUP) * pairs, :] = jnp.dot(stack, right_w[m], preferred_element_type=F32)
            for p in range(pairs):
                dst[:, base + p * wide:base + (p + 1) * wide] = gather[pl.ds(p, QB, stride=pairs), :].astype(BF16)

    def to_partner(rows):
        return pltpu.make_async_remote_copy(
            vis.at[SELF, rows], vis.at[PARTNER, rows], near_send, near_recv,
            device_id=(partner, g), device_id_type=MESH)

    def to_cross(t):
        return pltpu.make_async_remote_copy(
            vis.at[SELF, rows_of(t)], vis.at[CROSS, rows_of(t)], far_send, far_recv.at[t],
            device_id=(cross, g), device_id_type=MESH)

    widths = [depth // fraction for fraction in PIECES]
    cuts = [slice(sum(widths[:k]), sum(widths[:k + 1])) for k in range(len(widths))]

    def tail_piece(k):
        at = rows_of(n_chunk - 1), cuts[k]
        return pltpu.make_async_remote_copy(
            vis.at[(SELF,) + at], vis.at[(CROSS,) + at], far_send, tail_recv.at[k],
            device_id=(cross, g), device_id_type=MESH)

    def prepare(i, carry):
        t = lax.rem(i + 1, n_chunk)
        load_raw(t).wait()
        precondition(raw.at[rows_of(t)], vis.at[SELF, rows_of(t)])

        @pl.when(jnp.logical_and(t > 0, t < n_chunk - 1))
        def _():
            to_cross(t).start()

        @pl.when(t == n_chunk - 1)
        def _():
            for k in range(len(cuts)):
                tail_piece(k).start()

        to_partner(rows_of(t)).start()
        return carry

    lax.fori_loop(0, n_chunk, prepare, 0)
    slab_copy.wait()

    def to_hop(w, t):
        d, rel, to_x, j = order(t)
        return pltpu.make_async_remote_copy(
            part.at[w, rows_of(t)], hop.at[w, rel, n_x - 1 - d], hop_send.at[w], hop_recv.at[w, rel],
            device_id=(b, yl * n_x + to_x), device_id_type=MESH)

    spans = [slice(at, at + SPAN) for at in range(0, depth, SPAN)]

    def score_all(w):
        for at in spans:
            product = nt_dot(vis[w, :, at], slab[:, at])
            part[w] = product if at.start == 0 else part[w] + product

        def send(t, carry):
            to_hop(w, t).start()
            return carry

        lax.fori_loop(0, n_chunk - 2, send, 0)

    def far(t):
        rows = rows_of(t)
        part[CROSS, rows] = sum(nt_dot(vis[CROSS, rows, at], slab[:, at]) for at in spans)

    def far_pieces(t):
        rows = rows_of(t)
        for k, at in enumerate(cuts):
            tail_piece(k).wait_recv()
            product = nt_dot(vis[CROSS, rows, at], slab[:, at])
            part[CROSS, rows] = product if k == 0 else part[CROSS, rows] + product

    def far_step(t, carry):
        @pl.when(t > 0)
        def _():
            to_cross(t).wait_recv()

        far(t)

        @pl.when(t < n_chunk - 2)
        def _():
            to_hop(CROSS, t).start()

        return carry

    owner = (b, partner, cross)

    def to_last(w, rel):
        return pltpu.make_async_remote_copy(
            mine.at[w, rel], last.at[w, rel], last_send.at[min(w, 1)], last_recv.at[w],
            device_id=(owner[w], g if rel == 0 else other), device_id_type=MESH)

    def group(ref, send, recv):
        return pltpu.make_async_remote_copy(
            ref, ref, send, recv, device_id=(partner, g), device_id_type=MESH)

    def gather_x(w, rel):
        group(hop.at[w, rel], hop_send.at[w], hop_recv.at[w, rel]).wait_recv()
        rows = rows_of(n_chunk - 2 + rel)
        total = part[w, rows]
        for d in range(n_x - 1):
            total = total + hop[w, rel, d]
        if w == SELF and rel == 0:
            part[w, rows] = total
        else:
            mine[w, rel] = total.astype(mine.dtype)
            to_last(w, rel).start()

    def finish(w):
        width = part.shape[2]
        if w == SELF:
            to_last(w, 1).wait_recv()
            total = part[w, rows_of(n_chunk - 2)] + last[w, 1].astype(F32)
            o_ref[1] = total * mask[0:1, width:2 * width]
            return
        group(last.at[w], last_send.at[1], last_recv.at[w]).wait_recv()
        total = last[w, 0].astype(F32) + last[w, 1].astype(F32)
        upper = par == (1 if w == CROSS else 0)

        @pl.when(upper)
        def _():
            o_ref[2] = total * mask[0:1, 2 * width:3 * width]

        @pl.when(jnp.logical_not(upper))
        def _():
            o_ref[0] = total * mask[0:1, 0:width]

    score_all(SELF)
    to_partner(slice(None)).wait_recv()
    score_all(PARTNER)

    raw_out.wait_recv()
    precondition(vraw, vis.at[CROSS, rows_of(0)])
    lax.fori_loop(0, n_chunk - 1, far_step, 0)
    gather_x(CROSS, 0)
    far_pieces(n_chunk - 1)
    gather_x(CROSS, 1)
    for w in (SELF, PARTNER):
        for rel in range(2):
            gather_x(w, rel)
    finish(SELF)
    finish(PARTNER)

    raw_out.wait_send()
    to_partner(slice(None)).wait_send()
    group(vis.at[SELF, 0:(n_chunk - 1) * QB], far_send, far_recv.at[0]).wait_send()
    for w in range(3):
        group(part.at[w, 0:(n_chunk - 2) * QB], hop_send.at[w], hop_recv.at[w, 0]).wait_send()
    to_last(SELF, 1).wait_send()
    group(mine.at[1:3], last_send.at[1], last_recv.at[1]).wait_send()
    finish(CROSS)


def solution(mesh):
    n_ex = mesh.shape["ex"]
    n_grp = mesh.shape["grp"]
    n_x = n_grp // 2

    def body(queries, inv_in, inv_out, store, listed):
        count, dims = queries.shape
        examples = store.shape[0]
        n_chunk = count // QB
        modules, side, _ = inv_in.shape
        tile = (QB, examples)
        vmem = pl.BlockSpec(memory_space=pltpu.VMEM)
        hbm = pl.BlockSpec(memory_space=pltpu.HBM)
        dma = pltpu.SemaphoreType.DMA
        return pl.pallas_call(
            functools.partial(kernel, n_ex, n_x),
            out_shape=jax.ShapeDtypeStruct((3,) + tile, F32),
            in_specs=[hbm] * 5,
            out_specs=vmem,
            scratch_shapes=[
                pltpu.VMEM(inv_in.shape, BF16),
                pltpu.VMEM(inv_out.shape, BF16),
                pltpu.VMEM(listed.shape, listed.dtype),
                pltpu.VMEM((count, dims), BF16),
                pltpu.VMEM((QB, dims), BF16),
                pltpu.VMEM((3, count, dims), BF16),
                pltpu.VMEM((examples, dims), BF16),
                pltpu.VMEM((3, count, examples), F32),
                pltpu.VMEM((3, 2, n_x - 1) + tile, F32),
                pltpu.VMEM((3, 2) + tile, BF16),
                pltpu.VMEM((3, 2) + tile, BF16),
                pltpu.VMEM((modules, side, side), BF16),
                pltpu.VMEM((modules, 2 * side, 2 * side), BF16),
                pltpu.VMEM((QB * side // 2, 2 * side), F32),
                pltpu.VMEM((QB * side // 2, 2 * side), F32),
                pltpu.VMEM((listed.shape[0], listed.shape[1] * SUB), F32),
                dma((3,)),
                dma((n_chunk,)),
                dma,
                dma,
                dma,
                dma,
                dma,
                dma,
                dma((n_chunk,)),
                dma((len(PIECES),)),
                dma((3,)),
                dma((3, 2)),
                dma((2,)),
                dma((3,)),
            ],
            compiler_params=pltpu.CompilerParams(
                collective_id=0, has_side_effects=True, vmem_limit_bytes=36 * 2**20),
        )(*[pltpu.with_memory_space_constraint(v, pltpu.HBM) for v in (queries, inv_in, inv_out, store, listed)])

    in_specs = (
        P("ex", "grp"),
        P("grp", None, None),
        P("grp", None, None),
        P("ex", "grp"),
        P("ex", None),
    )
    out_specs = P(None, ("ex", "grp"), None)
    return jax.shard_map(body, mesh=mesh, in_specs=in_specs, out_specs=out_specs, check_vma=False)
```
